32 devices in a mesh: seq: 8 (over y, x, core), blk: 4 (over z).
Axes of the slice: x: 2, y: 2, z: 4, core: 2. Of those that a mesh axis runs over, the one named last changes fastest.
Arguments:
- states: bfloat16 [8, 2560, 768], P('seq', 'blk'), may hold values from -6 to 6
- cotangent: bfloat16 [8, 2560, 768], P('seq', 'blk'), may hold values from -6 to 6
- lengths: int32 [8, 5], P('seq'), may hold values from 64 to 512, as said below
- w_qkv: bfloat16 [768, 2304], P(('seq', 'blk')), may hold values from -0.21875 to 0.21875
- w_out: bfloat16 [768, 768], P(('seq', 'blk')), may hold values from -1.75 to 1.75
- w_up: bfloat16 [768, 3072], P(('seq', 'blk')), may hold values from -0.21875 to 0.21875
- w_down: bfloat16 [3072, 768], P(('seq', 'blk')), may hold values from -0.109375 to 0.109375
- vectors: bfloat16 [13, 768], P(None, ('seq', 'blk'))
- up_bias: bfloat16 [3072], P(('seq', 'blk')), may hold values from -1.796875 to 1.796875
Outputs:
- result: bfloat16 [8, 2560, 768], P('seq', 'blk')
- grad_states: bfloat16 [8, 2560, 768], P('seq', 'blk')
- grad_qkv: float32 [768, 2304], P(('seq', 'blk'))
- grad_out: float32 [768, 768], P(('seq', 'blk'))
- grad_up: float32 [768, 3072], P(('seq', 'blk'))
- grad_down: float32 [3072, 768], P(('seq', 'blk'))
- grad_vectors: float32 [13, 768], P(None, ('seq', 'blk'))
- grad_up_bias: float32 [3072], P(('seq', 'blk'))
The draws below stay inside these ranges and needn't reach their ends.
Inputs may be any that keep to these rules, and one draw needn't show every extreme that they name: `lengths`: every sequence's first pass has all 512 slots live; a later pass has between 64 and 512 live slots, the live ones first.
All inputs are finite; a program needn't handle non-finite values.
Results may differ from the reference program's by a relative error of at most 0.015.
Values may be sent and summed in bfloat16 or wider, within the bound.
No kernel may reach another device: no remote copies, remote signals or barrier semaphores. Data moves between devices by JAX's collectives and lax.ppermute only.
A program may use at most 192 MiB of HBM per device.

```python
import jax
import jax.numpy as jnp
from jax import lax

D = 768
HEADS = 12
HEAD = 64
FF = 3072
PASSES = 5
PASS_SLOTS = 512
MIN_LEN = 64
NV = 13
SEQS = 8
SLOTS = 2560


def draw_lengths(key, part):
    others = jax.random.randint(key, (SEQS, PASSES), MIN_LEN, PASS_SLOTS + 1, dtype=jnp.int32)
    first_pass = (jnp.arange(PASSES, dtype=jnp.int32) == 0)[None, :]
    return jnp.where(first_pass, PASS_SLOTS, others).astype(jnp.int32)


def draw_vectors(key, part):
    keys = jax.random.split(jax.random.fold_in(key, 7), 2)
    normal_part = jax.random.normal(keys[0], (NV, D), jnp.float32)
    gain_part = jax.random.uniform(keys[1], (NV, D), jnp.float32, 0.5, 1.5)
    spreads = jnp.array([0.5, 0.5, 0.5, 0.5, 0.5, 0.0, 0.3, 0.5, 0.5, 0.3, 0.0, 0.3, 0.3], jnp.float32)
    is_gain = jnp.array([0, 0, 0, 0, 0, 1, 0, 0, 0, 0, 1, 0, 0], jnp.float32)
    table = normal_part * spreads[:, None] + gain_part * is_gain[:, None]
    return table.astype(jnp.bfloat16)


def block_scale(stream_key, dims, pieces, smallest, high):
    def one(position, blocks):
        heights = jax.random.uniform(jax.random.fold_in(jax.random.fold_in(stream_key, 6), position), (blocks,), jnp.float32, smallest / len(pieces), high / len(pieces))
        return jnp.repeat(jnp.exp(heights), dims[position] // blocks).reshape((-1,) + (1,) * (len(dims) - position - 1))

    level = one(*pieces[0])
    for cut in pieces[1:]:
        level = level * one(*cut)
    return level


def centred(rng, extent, deviation, bound, cuts=(), kind=jnp.bfloat16):
    level = block_scale(rng, extent, cuts, -0.22, 0.18) if cuts else 1.0
    values = jax.random.normal(rng, extent, jnp.float32) * deviation * level
    return jnp.minimum(jnp.maximum(values, -bound), bound).astype(kind)


def setup_inputs(seed: int = 0) -> dict:
    splits = jax.random.split(jax.random.key(seed), 10)
    return {
        "states": centred(splits[0], (SEQS, SLOTS, D), 1.0, 6.0, ((0, 8), (1, 4))),
        "cotangent": centred(splits[1], (SEQS, SLOTS, D), 1.0, 6.0, ((0, 8), (1, 4))),
        "lengths": draw_lengths(jax.random.fold_in(splits[9], 71), 0),
        "w_qkv": centred(splits[3], (D, 3 * D), D ** -0.5, 0.21875, ((0, 32),)),
        "w_out": centred(splits[4], (D, D), (D // 64) ** -0.5, 1.75, ((0, 32),)),
        "w_up": centred(splits[5], (D, FF), D ** -0.5, 0.21875, ((0, 32),)),
        "w_down": centred(splits[6], (FF, D), FF ** -0.5, 0.109375, ((0, 32),)),
        "vectors": draw_vectors(jax.random.fold_in(splits[9], 71), 0),
        "up_bias": centred(splits[8], (FF,), 0.3, 1.796875, ((0, 32),)),
    }


highest = lax.Precision.HIGHEST
masked_value = -1e+30

@jax.custom_vjp
def low(v):
    return lax.optimization_barrier(v.astype(jnp.bfloat16)).astype(jnp.float32)

@jax.custom_vjp
def low_back(v):
    return v

def low_keep(v):
    return (low(v), None)

def low_pass(kept, grad):
    return (grad,)

def back_keep(v):
    return (v, None)

def back_low(kept, grad):
    return (low(grad),)
low.defvjp(low_keep, low_pass)
low_back.defvjp(back_keep, back_low)

def layer_norm(values, gain, offset):
    centre = values - lax.optimization_barrier(jnp.mean(values, axis=-1, keepdims=True))
    spread = lax.optimization_barrier(jnp.mean(centre * centre, axis=-1, keepdims=True))
    return centre * lax.rsqrt(spread + 1e-05) * gain + offset

def live_slots(slot_index, pass_lengths):
    matches = (slot_index // PASS_SLOTS)[:, None] == jnp.arange(PASSES, dtype=jnp.int32)[None, :]
    bounds = lax.optimization_barrier(jnp.sum(jnp.where(matches, pass_lengths[None, :], 0), axis=1))
    return slot_index % PASS_SLOTS < bounds

def visible(query_slots, key_slots, key_live):
    earlier = key_slots[None, :] // PASS_SLOTS <= query_slots[:, None] // PASS_SLOTS
    before = key_slots[None, :] % PASS_SLOTS <= query_slots[:, None] % PASS_SLOTS
    return earlier & before & key_live[None, :]

def attend_block(queries, query_slots, key_rows, value_rows, key_live):
    scores = low_back(jnp.einsum('qhe,khe->hqk', queries, key_rows, precision=highest) * 0.125)
    key_slots = jnp.arange(SLOTS, dtype=jnp.int32)
    visible_mask = visible(query_slots, key_slots, key_live)
    scores = jnp.where(visible_mask[None], scores, masked_value)
    chances = low(jax.nn.softmax(scores, axis=-1))
    return jnp.einsum('hqk,khe->qhe', chances, value_rows, precision=highest)

def forward(states, pass_lengths, w_qkv, w_out, w_up, w_down, vectors, up_bias):
    slot_index = jnp.arange(SLOTS, dtype=jnp.int32)
    slot_live = live_slots(slot_index, pass_lengths)
    live_weight = slot_live.astype(jnp.float32)[:, None]
    pass_table = ((slot_index // PASS_SLOTS)[:, None] == jnp.arange(PASSES, dtype=jnp.int32)[None, :]).astype(jnp.float32)
    start = states + jnp.dot(pass_table, vectors[:PASSES], precision=highest)
    normed_a = low(layer_norm(start, vectors[5], vectors[6]))
    bias_three = jnp.concatenate([vectors[7], jnp.zeros_like(vectors[7]), vectors[8]])
    projected = low(low_back(jnp.dot(normed_a, w_qkv, precision=highest) + bias_three))
    queries = projected[:, :D].reshape(PASSES, PASS_SLOTS, HEADS, HEAD)
    key_rows = projected[:, D:2 * D].reshape(SLOTS, HEADS, HEAD)
    value_rows = projected[:, 2 * D:].reshape(SLOTS, HEADS, HEAD)
    checked = jax.checkpoint(attend_block)

    def one_block(item):
        return checked(item[0], item[1], key_rows, value_rows, slot_live)
    mixture = lax.map(one_block, (queries, slot_index.reshape(PASSES, PASS_SLOTS))).reshape(SLOTS, D)
    heads_out = low(low_back(mixture))
    attn_branch = low_back(jnp.dot(heads_out, w_out, precision=highest) + vectors[9])
    middle = start + live_weight * attn_branch
    normed_b = low(layer_norm(middle, vectors[10], vectors[11]))
    up_sum = low_back(jnp.dot(normed_b, w_up, precision=highest) + up_bias)
    hidden = low(jax.nn.gelu(up_sum, approximate=True))
    ffn_branch = low_back(jnp.dot(hidden, w_down, precision=highest) + vectors[12])
    return middle + live_weight * ffn_branch

def reference(states, cotangent, lengths, w_qkv, w_out, w_up, w_down, vectors, up_bias):
    params = (w_qkv.astype(jnp.float32), w_out.astype(jnp.float32), w_up.astype(jnp.float32), w_down.astype(jnp.float32), vectors.astype(jnp.float32), up_bias.astype(jnp.float32))

    def step(totals, item):
        seq_states, seq_grads, pass_lengths = item

        def runner(state_arg, p_qkv, p_out, p_up, p_down, p_vectors, p_bias):
            return forward(state_arg, pass_lengths, p_qkv, p_out, p_up, p_down, p_vectors, p_bias)
        outcome, pull = jax.vjp(runner, seq_states.astype(jnp.float32), *params)
        gradients = pull(seq_grads.astype(jnp.float32))
        totals = tuple((prior + extra for prior, extra in zip(totals, gradients[1:])))
        return (totals, (outcome.astype(jnp.bfloat16), gradients[0].astype(jnp.bfloat16)))
    zeros = tuple((jnp.zeros_like(param) for param in params))
    totals, (outcomes, grad_states) = lax.scan(step, zeros, (states, cotangent, lengths))
    return (outcomes, grad_states, totals[0], totals[1], totals[2], totals[3], totals[4], totals[5])
```

```python
import functools

import jax
import jax.numpy as jnp
from jax import lax
from jax.experimental import pallas as pl
from jax.experimental.pallas import tpu as pltpu
from jax.sharding import PartitionSpec as P

HEAD = 64
PASSES = 5
PASS_SLOTS = 512

masked_value = -1e30
both = ("seq", "blk")
f32 = jnp.float32
bf16 = jnp.bfloat16


def layer_norm(values, gain, offset):
    centre = values - jnp.mean(values, axis=-1, keepdims=True)
    spread = jnp.mean(centre * centre, axis=-1, keepdims=True)
    return centre * lax.rsqrt(spread + 1e-05) * gain + offset


def gelu_tanh(values):
    return jax.nn.gelu(values, approximate=True)


def contract(left, right, dims):
    return lax.dot_general(left, right, (dims, ((), ())), preferred_element_type=f32)


def tile_visible(length):
    key_place = lax.broadcasted_iota(jnp.int32, (PASS_SLOTS, PASS_SLOTS), 0)
    query_place = lax.broadcasted_iota(jnp.int32, (PASS_SLOTS, PASS_SLOTS), 1)
    return (key_place <= query_place) & (key_place < length)


def head_only(rows, head):
    lanes = lax.broadcasted_iota(jnp.int32, rows.shape, 1)
    return jnp.where(lanes // HEAD == head, rows, jnp.zeros_like(rows))


def forward_kernel(lengths, packed, out, totals, value_t):
    width = out.shape[1]
    heads = width // HEAD
    value_t[...] = packed[:, 2 * width :].astype(f32).T.astype(bf16)

    def query_pass(query_index, _):
        query_rows = pl.ds(query_index * PASS_SLOTS, PASS_SLOTS)
        queries = packed[query_rows, :width]
        queries = [head_only(queries, h) * jnp.asarray(0.125, bf16) for h in range(heads)]

        def key_pass(key_index, carried):
            start = pl.multiple_of(key_index * PASS_SLOTS, PASS_SLOTS)
            key_rows = pl.ds(start, PASS_SLOTS)
            keys = packed[key_rows, width : 2 * width]
            shown = tile_visible(lengths[0, key_index])
            updated = []
            for h in range(heads):
                top, total, acc = carried[h]
                scores = contract(keys, queries[h], ((1,), (1,)))
                scores = jnp.where(shown, scores, masked_value)
                newest = jnp.maximum(top, jnp.max(scores, axis=0, keepdims=True))
                shares = jnp.exp(scores - newest)
                fade = jnp.exp(top - newest)
                total = total * fade + jnp.sum(shares, axis=0, keepdims=True)
                values = value_t[h * HEAD : (h + 1) * HEAD, key_rows]
                acc = acc * fade + contract(values, shares.astype(bf16), ((1,), (0,)))
                updated.append((newest, total, acc))
            return tuple(updated)

        empty = (
            jnp.full((1, PASS_SLOTS), masked_value, f32),
            jnp.zeros((1, PASS_SLOTS), f32),
            jnp.zeros((HEAD, PASS_SLOTS), f32),
        )
        found = lax.fori_loop(0, query_index + 1, key_pass, (empty,) * heads)
        mixed = jnp.concatenate([acc / total for _, total, acc in found], axis=0)
        out[query_rows, :] = mixed.T.astype(bf16)
        for h, (top, total, _) in enumerate(found):
            totals[pl.ds(query_index, 1), h, :] = top + jnp.log(total)
        return 0

    lax.fori_loop(0, PASSES, query_pass, 0)


def backward_kernel(lengths, packed, mixed, grad, totals, out, grad_query, grad_key, grad_value):
    width = mixed.shape[1]
    heads = width // HEAD
    grad_query[...] = jnp.zeros_like(grad_query)
    eighth = jnp.asarray(0.125, bf16)

    def key_pass(key_index, _):
        key_rows = pl.ds(pl.multiple_of(key_index * PASS_SLOTS, PASS_SLOTS), PASS_SLOTS)
        keys = packed[key_rows, width : 2 * width] * eighth
        values = packed[key_rows, 2 * width :]
        keys = [head_only(keys, h) for h in range(heads)]
        values = [head_only(values, h) for h in range(heads)]
        shown = tile_visible(lengths[0, key_index])
        grad_key[...] = jnp.zeros_like(grad_key)
        grad_value[...] = jnp.zeros_like(grad_value)

        def query_pass(query_index, _):
            query_rows = pl.ds(pl.multiple_of(query_index * PASS_SLOTS, PASS_SLOTS), PASS_SLOTS)
            queries = packed[query_rows, :width]
            grads = grad[query_rows, :]
            product = (grads.astype(f32) * mixed[query_rows, :].astype(f32)).T
            scaled = queries * eighth
            add_query = add_key = add_value = 0.0
            for h in range(heads):
                delta = jnp.sum(product[h * HEAD : (h + 1) * HEAD], axis=0, keepdims=True)
                scores = contract(keys[h], queries, ((1,), (1,)))
                total = totals[pl.ds(query_index, 1), h, :]
                shares = jnp.where(shown, jnp.exp(scores - total), 0.0)
                grad_shares = contract(values[h], grads, ((1,), (1,)))
                grad_scores = (shares * (grad_shares - delta)).astype(bf16)
                add_value += contract(shares.astype(bf16), head_only(grads, h), ((1,), (0,)))
                add_key += contract(grad_scores, head_only(scaled, h), ((1,), (0,)))
                add_query += contract(grad_scores, keys[h], ((0,), (0,)))
            grad_query[query_rows, :] += add_query
            grad_key[...] += add_key
            grad_value[...] += add_value
            return 0

        lax.fori_loop(key_index, PASSES, query_pass, 0)
        out[key_rows, width : 2 * width] = grad_key[...].astype(bf16)
        out[key_rows, 2 * width :] = grad_value[...].astype(bf16)
        return 0

    lax.fori_loop(0, PASSES, key_pass, 0)
    out[:, :width] = grad_query[...].astype(bf16)


in_vmem = functools.partial(pl.BlockSpec, memory_space=pltpu.VMEM)
in_smem = functools.partial(pl.BlockSpec, memory_space=pltpu.SMEM)


def attend(lengths, packed):
    slots, triple = packed.shape
    width = triple // 3
    return pl.pallas_call(
        forward_kernel,
        out_shape=(
            jax.ShapeDtypeStruct((slots, width), bf16),
            jax.ShapeDtypeStruct((PASSES, width // HEAD, PASS_SLOTS), f32),
        ),
        in_specs=[in_smem(), in_vmem()],
        out_specs=(in_vmem(), in_vmem()),
        scratch_shapes=[pltpu.VMEM((width, slots), bf16)],
        compiler_params=pltpu.CompilerParams(vmem_limit_bytes=48 << 20),
        name="attend",
    )(lengths, packed)


def attend_back(lengths, packed, mixed, grad, totals):
    slots, width = mixed.shape
    return pl.pallas_call(
        backward_kernel,
        out_shape=jax.ShapeDtypeStruct(packed.shape, bf16),
        in_specs=[in_smem(), in_vmem(), in_vmem(), in_vmem(), in_vmem()],
        out_specs=in_vmem(),
        scratch_shapes=[
            pltpu.VMEM((slots, width), f32),
            pltpu.VMEM((PASS_SLOTS, width), f32),
            pltpu.VMEM((PASS_SLOTS, width), f32),
        ],
        compiler_params=pltpu.CompilerParams(vmem_limit_bytes=48 << 20),
        name="attend_back",
    )(lengths, packed, mixed, grad, totals)


def by_group(rows, groups):
    count, triple = rows.shape
    return rows.reshape(count, 3, groups, -1).swapaxes(1, 2).reshape(count, triple)


def by_kind(rows, groups):
    count, triple = rows.shape
    return rows.reshape(count, groups, 3, -1).swapaxes(1, 2).reshape(count, triple)


def to_heads(rows):
    return lax.all_to_all(rows, "blk", 1, 0, tiled=True)


def to_slots(rows):
    return lax.all_to_all(rows, "blk", 0, 1, tiled=True)


def norm_back(values, gain, grad):
    centre = values - jnp.mean(values, axis=-1, keepdims=True)
    spread = jnp.mean(centre * centre, axis=-1, keepdims=True)
    scale = lax.rsqrt(spread + 1e-05)
    hat = centre * scale
    edge = grad * gain
    part = scale * (
        edge
        - jnp.mean(edge, axis=-1, keepdims=True)
        - hat * jnp.mean(edge * hat, axis=-1, keepdims=True)
    )
    return part, jnp.sum(grad * hat, axis=0), jnp.sum(grad, axis=0)


def on_device(states, cotangent, lengths, w_qkv, w_out, w_up, w_down, vectors, up_bias):
    _, row_count, width = states.shape
    groups = lax.axis_size("blk")
    own = w_qkv.shape[0]
    wide = w_up.shape[1]
    ratio = wide // width
    vector_count = vectors.shape[0]
    first = jnp.concatenate(
        [
            by_group(w_qkv, groups),
            vectors.T,
            up_bias.reshape(own, ratio),
            jnp.zeros((own, 128 - vector_count - ratio), bf16),
        ],
        axis=1,
    )
    first = lax.all_gather(first, both, axis=0, tiled=True)
    second = jnp.concatenate([w_out, w_up, w_down.reshape(own, wide)], axis=1)
    second, _ = lax.optimization_barrier((second, first[:8, :128]))
    second = lax.all_gather(second, both, axis=0, tiled=True)
    full_qkv = first[:, : 3 * width]
    table = first[:, 3 * width : 3 * width + vector_count].astype(f32).T
    bias_up = first[:, 3 * width + vector_count : 3 * width + vector_count + ratio]
    bias_up = bias_up.astype(f32).reshape(wide)
    full_out = second[:, :width]
    full_up = second[:, width : width + wide]
    full_down = second[:, width + wide :].reshape(wide, width)

    slots = lax.axis_index("blk") * row_count + jnp.arange(row_count, dtype=jnp.int32)
    pass_of = (slots // PASS_SLOTS)[:, None] == jnp.arange(PASSES, dtype=jnp.int32)[None, :]
    bounds = jnp.sum(jnp.where(pass_of, lengths[0][None, :], 0), axis=1)
    live = (slots % PASS_SLOTS < bounds).astype(f32)[:, None]
    pass_table = pass_of.astype(f32)

    added = jnp.zeros((row_count, width), f32)
    for index in range(PASSES):
        added = jnp.where(pass_of[:, index : index + 1], table[index], added)
    start = states[0].astype(f32) + added
    normed_a = layer_norm(start, table[5], table[6]).astype(bf16)
    bias_three = jnp.concatenate([table[7], jnp.zeros_like(table[7]), table[8]])
    bias_three = by_group(bias_three[None], groups)
    projected = (contract(normed_a, full_qkv, ((1,), (0,))) + bias_three).astype(bf16)
    packed = to_heads(projected)
    mixed, totals = attend(lengths, packed)
    heads_out = to_slots(mixed)
    middle = start + live * (contract(heads_out, full_out, ((1,), (0,))) + table[9])
    normed_b = layer_norm(middle, table[10], table[11]).astype(bf16)
    up_sum = contract(normed_b, full_up, ((1,), (0,))) + bias_up
    activated, gelu_pull = jax.vjp(gelu_tanh, up_sum)
    hidden = activated.astype(bf16)
    outcome = middle + live * (contract(hidden, full_down, ((1,), (0,))) + table[12])

    incoming = cotangent[0].astype(f32)
    grad_branch = (live * incoming).astype(bf16)
    grad_down = contract(hidden, grad_branch, ((0,), (0,)))
    grad_hidden = contract(grad_branch, full_down, ((1,), (1,)))
    grad_upsum = gelu_pull(grad_hidden)[0].astype(bf16)
    grad_up = contract(normed_b, grad_upsum, ((0,), (0,)))
    grad_normb = contract(grad_upsum, full_up, ((1,), (1,)))
    middle_part, gain_grad_b, shift_grad_b = norm_back(middle, table[10], grad_normb)
    grad_middle = incoming + middle_part
    grad_attn = (live * grad_middle).astype(bf16)
    grad_out = contract(heads_out, grad_attn, ((0,), (0,)))
    grad_heads = contract(grad_attn, full_out, ((1,), (1,))).astype(bf16)
    late = jnp.concatenate(
        [grad_out.astype(bf16), grad_up.astype(bf16), grad_down.astype(bf16).reshape(width, wide)],
        axis=1,
    )
    late = lax.psum_scatter(late, both, scatter_dimension=0, tiled=True)

    grad_packed = attend_back(lengths, packed, mixed, to_heads(grad_heads), totals)
    grad_projected = to_slots(grad_packed)
    grad_qkv = contract(normed_a, grad_projected, ((0,), (0,)))
    column_sums = by_kind(jnp.sum(grad_projected.astype(f32), axis=0)[None], groups)[0]
    grad_norma = contract(grad_projected, full_qkv, ((1,), (1,)))
    start_part, gain_grad_a, shift_grad_a = norm_back(start, table[5], grad_norma)
    grad_start = grad_middle + start_part
    grad_embed = [
        jnp.sum(jnp.where(pass_of[:, index : index + 1], grad_start, 0.0), axis=0)
        for index in range(PASSES)
    ]
    vector_grads = jnp.stack(
        grad_embed
        + [
            gain_grad_a,
            shift_grad_a,
            column_sums[:width],
            column_sums[2 * width :],
            jnp.sum(grad_attn.astype(f32), axis=0),
            gain_grad_b,
            shift_grad_b,
            jnp.sum(grad_branch.astype(f32), axis=0),
        ]
    )
    bias_grads = jnp.sum(grad_upsum.astype(f32), axis=0)
    last = jnp.concatenate(
        [
            grad_qkv.astype(bf16),
            vector_grads.T.astype(bf16),
            bias_grads.reshape(width, ratio).astype(bf16),
            jnp.zeros((width, 128 - vector_count - ratio), bf16),
        ],
        axis=1,
    )
    last = lax.psum_scatter(last, both, scatter_dimension=0, tiled=True).astype(f32)
    late = late.astype(f32)
    edge = 3 * width + vector_count
    return (
        outcome.astype(bf16)[None],
        grad_start.astype(bf16)[None],
        by_kind(last[:, : 3 * width], groups),
        late[:, :width],
        late[:, width : width + wide],
        late[:, width + wide :].reshape(own * ratio, width),
        last[:, 3 * width : edge].T,
        last[:, edge : edge + ratio].reshape(own * ratio),
    )


def solution(mesh):
    split = P(both, None)
    return jax.shard_map(
        on_device,
        mesh=mesh,
        in_specs=(
            P("seq", "blk", None),
            P("seq", "blk", None),
            P("seq", None),
            split,
            split,
            split,
            split,
            P(None, both),
            P(both),
        ),
        out_specs=(
            P("seq", "blk", None),
            P("seq", "blk", None),
            split,
            split,
            split,
            split,
            P(None, both),
            P(both),
        ),
        check_vma=False,
    )
```

```python
import functools

import jax
import jax.numpy as jnp
from jax import lax
from jax.experimental import pallas as pl
from jax.experimental.layout import Layout, with_layout_constraint
from jax.experimental.pallas import tpu as pltpu
from jax.sharding import PartitionSpec as P

HEAD = 64
PASSES = 5
PASS_SLOTS = 512
SPLIT = 2

masked_value = -1e30
both = ("seq", "blk")
f32 = jnp.float32
bf16 = jnp.bfloat16


def layer_norm(values, gain, offset):
    centre = values - jnp.mean(values, axis=-1, keepdims=True)
    spread = jnp.mean(centre * centre, axis=-1, keepdims=True)
    return centre * lax.rsqrt(spread + 1e-05) * gain + offset


def gelu_tanh(values):
    return jax.nn.gelu(values, approximate=True)


def contract(left, right, dims):
    return lax.dot_general(left, right, (dims, ((), ())), preferred_element_type=f32)


def tile_visible(length):
    key_place = lax.broadcasted_iota(jnp.int32, (PASS_SLOTS, PASS_SLOTS), 0)
    query_place = lax.broadcasted_iota(jnp.int32, (PASS_SLOTS, PASS_SLOTS), 1)
    return (key_place <= query_place) & (key_place < length)


def head_only(rows, head):
    lanes = lax.broadcasted_iota(jnp.int32, rows.shape, 1)
    return jnp.where(lanes // HEAD == head, rows, jnp.zeros_like(rows))


def place_pieces(here, pieces, whole):
    rows = pieces[0].shape[0]
    for step, piece in enumerate(pieces):
        at = pl.multiple_of((here ^ step) * rows, rows)
        whole[pl.ds(at, rows), :] = piece[...]


def forward_kernel(lengths, here, *refs):
    packed, out, totals, value_t = refs[-4:]
    width = out.shape[1]
    heads = width // HEAD
    place_pieces(here[0], refs[:-4], packed)
    value_t[...] = packed[:, 2 * width :].astype(f32).T.astype(bf16)

    def query_pass(query_index, _):
        query_rows = pl.ds(query_index * PASS_SLOTS, PASS_SLOTS)
        queries = packed[query_rows, :width]
        queries = [head_only(queries, h) * jnp.asarray(0.125, bf16) for h in range(heads)]

        def key_pass(key_index, carried):
            start = pl.multiple_of(key_index * PASS_SLOTS, PASS_SLOTS)
            key_rows = pl.ds(start, PASS_SLOTS)
            keys = packed[key_rows, width : 2 * width]
            shown = tile_visible(lengths[0, key_index])
            updated = []
            for h in range(heads):
                top, total, acc = carried[h]
                scores = contract(keys, queries[h], ((1,), (1,)))
                scores = jnp.where(shown, scores, masked_value)
                newest = jnp.maximum(top, jnp.max(scores, axis=0, keepdims=True))
                shares = jnp.exp(scores - newest)
                fade = jnp.exp(top - newest)
                total = total * fade + jnp.sum(shares, axis=0, keepdims=True)
                values = value_t[h * HEAD : (h + 1) * HEAD, key_rows]
                acc = acc * fade + contract(values, shares.astype(bf16), ((1,), (0,)))
                updated.append((newest, total, acc))
            return tuple(updated)

        empty = (
            jnp.full((1, PASS_SLOTS), masked_value, f32),
            jnp.zeros((1, PASS_SLOTS), f32),
            jnp.zeros((HEAD, PASS_SLOTS), f32),
        )
        found = lax.fori_loop(0, query_index + 1, key_pass, (empty,) * heads)
        mixed = jnp.concatenate([acc / total for _, total, acc in found], axis=0)
        out[query_rows, :] = mixed.T.astype(bf16)
        for h, (top, total, _) in enumerate(found):
            totals[pl.ds(query_index, 1), h, :] = top + jnp.log(total)
        return 0

    lax.fori_loop(0, PASSES, query_pass, 0)


def first_backward_kernel(lengths, here, packed, mixed, totals, *refs):
    out, grad, grad_query, grad_key, grad_value = refs[-5:]
    place_pieces(here[0], refs[:-5], grad)
    grad_query[...] = jnp.zeros_like(grad_query)
    backward_passes(
        0, SPLIT, lengths, packed, mixed, grad, totals, out, grad_query, grad_key, grad_value
    )


def second_backward_kernel(
    lengths, packed, mixed, totals, grad, begun, query_in, out, grad_query, grad_key, grad_value
):
    width = mixed.shape[1]
    grad_query[...] = query_in[...]
    out[: SPLIT * PASS_SLOTS, width:] = begun[...]
    backward_passes(
        SPLIT, PASSES, lengths, packed, mixed, grad, totals, out, grad_query, grad_key, grad_value
    )
    out[:, :width] = grad_query[...].astype(bf16)


def backward_passes(
    first, last, lengths, packed, mixed, grad, totals, out, grad_query, grad_key, grad_value
):
    width = mixed.shape[1]
    heads = width // HEAD
    offset = out.shape[1] - 3 * width
    eighth = jnp.asarray(0.125, bf16)

    def key_pass(key_index, _):
        key_rows = pl.ds(pl.multiple_of(key_index * PASS_SLOTS, PASS_SLOTS), PASS_SLOTS)
        keys = packed[key_rows, width : 2 * width] * eighth
        values = packed[key_rows, 2 * width :]
        keys = [head_only(keys, h) for h in range(heads)]
        values = [head_only(values, h) for h in range(heads)]
        shown = tile_visible(lengths[0, key_index])
        grad_key[...] = jnp.zeros_like(grad_key)
        grad_value[...] = jnp.zeros_like(grad_value)

        def query_pass(query_index, _):
            query_rows = pl.ds(pl.multiple_of(query_index * PASS_SLOTS, PASS_SLOTS), PASS_SLOTS)
            queries = packed[query_rows, :width]
            grads = grad[query_rows, :]
            product = (grads.astype(f32) * mixed[query_rows, :].astype(f32)).T
            scaled = queries * eighth
            add_query = add_key = add_value = 0.0
            for h in range(heads):
                delta = jnp.sum(product[h * HEAD : (h + 1) * HEAD], axis=0, keepdims=True)
                scores = contract(keys[h], queries, ((1,), (1,)))
                total = totals[pl.ds(query_index, 1), h, :]
                shares = jnp.where(shown, jnp.exp(scores - total), 0.0)
                grad_shares = contract(values[h], grads, ((1,), (1,)))
                grad_scores = (shares * (grad_shares - delta)).astype(bf16)
                add_value += contract(shares.astype(bf16), head_only(grads, h), ((1,), (0,)))
                add_key += contract(grad_scores, head_only(scaled, h), ((1,), (0,)))
                add_query += contract(grad_scores, keys[h], ((0,), (0,)))
            grad_query[query_rows, :] += add_query
            grad_key[...] += add_key
            grad_value[...] += add_value
            return 0

        lax.fori_loop(key_index, PASSES, query_pass, 0)
        out[key_rows, width + offset : 2 * width + offset] = grad_key[...].astype(bf16)
        out[key_rows, 2 * width + offset :] = grad_value[...].astype(bf16)
        return 0

    lax.fori_loop(first, last, key_pass, 0)


in_vmem = functools.partial(pl.BlockSpec, memory_space=pltpu.VMEM)
in_smem = functools.partial(pl.BlockSpec, memory_space=pltpu.SMEM)


def attend(lengths, here, pieces):
    rows, triple = pieces[0].shape
    slots = rows * len(pieces)
    width = triple // 3
    return pl.pallas_call(
        forward_kernel,
        out_shape=(
            jax.ShapeDtypeStruct((slots, triple), bf16),
            jax.ShapeDtypeStruct((slots, width), bf16),
            jax.ShapeDtypeStruct((PASSES, width // HEAD, PASS_SLOTS), f32),
        ),
        in_specs=[in_smem(), in_smem()] + [in_vmem()] * len(pieces),
        out_specs=(in_vmem(), in_vmem(), in_vmem()),
        scratch_shapes=[pltpu.VMEM((width, slots), bf16)],
        compiler_params=pltpu.CompilerParams(vmem_limit_bytes=48 << 20),
        name="attend",
    )(lengths, here, *pieces)


def attend_back_first(lengths, here, packed, mixed, totals, pieces):
    slots, width = mixed.shape
    return pl.pallas_call(
        first_backward_kernel,
        out_shape=(
            jax.ShapeDtypeStruct((SPLIT * PASS_SLOTS, 2 * width), bf16),
            jax.ShapeDtypeStruct((slots, width), bf16),
            jax.ShapeDtypeStruct((slots, width), f32),
        ),
        in_specs=[in_smem(), in_smem()] + [in_vmem()] * (3 + len(pieces)),
        out_specs=(in_vmem(), in_vmem(), in_vmem()),
        scratch_shapes=[
            pltpu.VMEM((PASS_SLOTS, width), f32),
            pltpu.VMEM((PASS_SLOTS, width), f32),
        ],
        compiler_params=pltpu.CompilerParams(vmem_limit_bytes=48 << 20),
        name="attend_back_first",
    )(lengths, here, packed, mixed, totals, *pieces)


def attend_back_second(lengths, packed, mixed, totals, grad, begun, query_in):
    slots, width = mixed.shape
    return pl.pallas_call(
        second_backward_kernel,
        out_shape=jax.ShapeDtypeStruct(packed.shape, bf16),
        in_specs=[in_smem()] + [in_vmem()] * 6,
        out_specs=in_vmem(),
        scratch_shapes=[
            pltpu.VMEM((slots, width), f32),
            pltpu.VMEM((PASS_SLOTS, width), f32),
            pltpu.VMEM((PASS_SLOTS, width), f32),
        ],
        compiler_params=pltpu.CompilerParams(vmem_limit_bytes=48 << 20),
        name="attend_back_second",
    )(lengths, packed, mixed, totals, grad, begun, query_in)


def row_major(values):
    return with_layout_constraint(values, Layout(tuple(range(values.ndim))))


def after(values, *others):
    return lax.optimization_barrier((values, others))[0]


def swap_with(values, axis, step):
    size = lax.axis_size(axis)
    return lax.ppermute(values, axis, [(i, i ^ step) for i in range(size)])


def axis_bits(axis):
    size = lax.axis_size(axis)
    assert size & (size - 1) == 0
    return [(axis, 1 << n) for n in reversed(range(size.bit_length() - 1))]


def bit_order(flip):
    places = axis_bits("seq") + axis_bits("blk")
    near = axis_bits("seq")
    far = near[:-1][::-1] if flip else near[:-1]
    return places, axis_bits("blk") + far + near[-1:]


def own_bit(bit):
    return (lax.axis_index(bit[0]) & bit[1]) != 0


class Gather:
    def __init__(self, piece, flip):
        self.places, self.order = bit_order(flip)
        self.shape = piece.shape
        self.piece = piece
        self.done = []

    def grow(self, count=None):
        count = len(self.order) if count is None else count
        for bit in self.order[:count]:
            other = swap_with(self.piece, *bit)
            self.done = sorted(self.done + [bit], key=self.places.index)
            mine = own_bit(bit)
            low = jnp.where(mine, other, self.piece)
            high = jnp.where(mine, self.piece, other)
            self.piece = jnp.stack([low, high], axis=self.done.index(bit))
        self.order = self.order[count:]
        return self.piece

    def whole(self):
        return self.grow().reshape((-1,) + self.shape[1:])


class Scatter:
    def __init__(self, whole, flip):
        self.left, order = bit_order(flip)
        self.order = order[::-1]
        rows = whole.shape[0] >> len(order)
        self.piece = whole.reshape((2,) * len(order) + (rows,) + whole.shape[1:])

    def send(self):
        bit, self.order = self.order[0], self.order[1:]
        at = self.left.index(bit)
        self.left = [place for place in self.left if place != bit]
        low = lax.index_in_dim(self.piece, 0, at, keepdims=False)
        high = lax.index_in_dim(self.piece, 1, at, keepdims=False)
        mine = own_bit(bit)
        self.bit = bit
        self.sent = jnp.where(mine, low, high)
        self.kept = jnp.where(mine, high, low)
        return (self.sent, self.kept)

    def receive(self):
        other = swap_with(self.sent, *self.bit)
        self.piece = (self.kept.astype(f32) + other.astype(f32)).astype(bf16)

    def finish(self):
        while self.order:
            self.send()
            self.receive()
        return self.piece


def swap_pieces(pieces):
    return [swap_with(piece, "blk", step) if step else piece for step, piece in enumerate(pieces)]


def in_order(pieces):
    here = lax.axis_index("blk")
    result = jnp.zeros((len(pieces),) + pieces[0].shape, pieces[0].dtype)
    for step, piece in enumerate(pieces):
        result = lax.dynamic_update_index_in_dim(result, piece, here ^ step, 0)
    return result


def at_group(values, group):
    return lax.dynamic_index_in_dim(values, group, 0, keepdims=False)


def by_group(rows, groups):
    count, triple = rows.shape
    rows = rows.reshape(count, 3, groups, -1)
    return [rows[:, :, g].reshape(count, triple // groups) for g in range(groups)]


def by_kind(parts):
    count, columns = parts[0].shape
    parts = [part.reshape(count, 3, columns // 3) for part in parts]
    return jnp.concatenate(parts, axis=2).reshape(count, -1)


def norm_parts(values):
    centre = values - jnp.mean(values, axis=-1, keepdims=True)
    spread = jnp.mean(centre * centre, axis=-1, keepdims=True)
    scale = lax.rsqrt(spread + 1e-05)
    return centre * scale, scale


def norm_back(values, gain, grad):
    hat, scale = norm_parts(values)
    edge = grad * gain
    part = scale * (
        edge
        - jnp.mean(edge, axis=-1, keepdims=True)
        - hat * jnp.mean(edge * hat, axis=-1, keepdims=True)
    )
    return part, jnp.sum(grad * hat, axis=0), jnp.sum(grad, axis=0)


def on_device(states, cotangent, lengths, w_qkv, w_out, w_up, w_down, vectors, up_bias):
    _, row_count, width = states.shape
    groups = lax.axis_size("blk")
    own = w_qkv.shape[0]
    wide = w_up.shape[1]
    ratio = wide // width
    vector_count = vectors.shape[0]
    share = width // groups
    span = 3 * share
    small = vector_count + ratio

    parts = by_group(w_qkv, groups)
    half = groups // 2
    extra = [vectors.T, up_bias.reshape(own, ratio), jnp.zeros((own, -small % 128), bf16)]
    here = lax.axis_index("blk").astype(jnp.int32)
    streams = [
        Gather(jnp.concatenate(parts[:half] + extra, axis=1), False),
        Gather(jnp.concatenate(parts[half:], axis=1), True),
    ]
    blk_steps = len(axis_bits("blk"))
    begun = [stream.grow(blk_steps) for stream in streams]
    w_out, w_up, w_down = after((w_out, w_up, w_down), begun)
    later = [Gather(w_up, False), Gather(w_down, True), Gather(w_out, False)]
    for one in later:
        one.grow(blk_steps)
    first = [stream.whole() for stream in streams]
    for one in later:
        one.piece = after(one.piece, first)
        one.grow(1)
    full_qkv = jnp.stack(
        [part[:, g * span : (g + 1) * span] for part in first for g in range(half)]
    )
    corner = first[0][:, half * span : half * span + small]
    table = corner[:, :vector_count].astype(f32).T
    bias_up = corner[:, vector_count:].astype(f32).reshape(wide)

    slots = lax.axis_index("blk") * row_count + jnp.arange(row_count, dtype=jnp.int32)
    pass_of = (slots // PASS_SLOTS)[:, None] == jnp.arange(PASSES, dtype=jnp.int32)[None, :]
    bounds = jnp.sum(jnp.where(pass_of, lengths[0][None, :], 0), axis=1)
    live = (slots % PASS_SLOTS < bounds).astype(f32)[:, None]

    added = jnp.zeros((row_count, width), f32)
    for index in range(PASSES):
        added = jnp.where(pass_of[:, index : index + 1], table[index], added)
    start = states[0].astype(f32) + added
    normed_a = layer_norm(start, table[5], table[6]).astype(bf16)
    bias_three = jnp.concatenate([table[7], jnp.zeros_like(table[7]), table[8]])
    bias_three = jnp.stack(by_group(bias_three[None], groups))

    def project(group):
        rows = contract(normed_a, at_group(full_qkv, group), ((1,), (0,)))
        return (rows + at_group(bias_three, group)).astype(bf16)

    pieces = [row_major(project(here ^ step)) for step in range(groups)]
    for one in later:
        one.piece = after(one.piece, pieces)
    full_up, full_down, full_out = [one.whole() for one in later]
    packed, mixed, totals = attend(lengths, here[None], swap_pieces(pieces))
    grouped = mixed.reshape(groups, row_count, share)
    pieces = swap_pieces([at_group(grouped, here ^ step) for step in range(groups)])
    heads_out = in_order(pieces)
    heads_out = jnp.concatenate([heads_out[g] for g in range(groups)], axis=1)
    middle = start + live * (contract(heads_out, full_out, ((1,), (0,))) + table[9])
    normed_b = layer_norm(middle, table[10], table[11]).astype(bf16)
    up_sum = contract(normed_b, full_up, ((1,), (0,))) + bias_up
    activated, gelu_pull = jax.vjp(gelu_tanh, up_sum)
    hidden = activated.astype(bf16)
    incoming = cotangent[0].astype(f32)
    grad_branch = (live * incoming).astype(bf16)
    grad_hidden = contract(grad_branch, full_down, ((1,), (1,)))
    grad_upsum = gelu_pull(grad_hidden)[0].astype(bf16)
    grad_normb = contract(grad_upsum, full_up, ((1,), (1,)))
    middle_part, gain_grad_b, shift_grad_b = norm_back(middle, table[10], grad_normb)
    grad_middle = incoming + middle_part
    grad_attn = (live * grad_middle).astype(bf16)
    out_rows = full_out.reshape(groups, share, width)

    def to_mixture(group):
        return contract(grad_attn, at_group(out_rows, group), ((1,), (1,))).astype(bf16)

    pieces = [row_major(to_mixture(here ^ step)) for step in range(groups)]
    hidden_late, grad_branch_late, grad_upsum_late, grad_attn_late = after(
        (hidden, grad_branch, grad_upsum, grad_attn), pieces
    )
    grad_down = contract(hidden_late, grad_branch_late, ((0,), (0,))).astype(bf16)
    grad_up = contract(normed_b, grad_upsum_late, ((0,), (0,))).astype(bf16)
    grad_out = contract(heads_out, grad_attn_late, ((0,), (0,))).astype(bf16)
    late = [Scatter(grad_down, True), Scatter(grad_up, False), Scatter(grad_out, False)]
    sent = [one.send() for one in late]
    pieces = after(swap_pieces(pieces), sent)
    for one in late:
        one.receive()
    done, grad_heads, grad_query = attend_back_first(
        lengths, here[None], packed, mixed, totals, pieces
    )
    for one in late:
        one.piece = after(one.piece, done)
    sent = [one.send() for one in late]
    grad_query = after(grad_query, sent)
    for one in late:
        one.receive()
    grad_packed = attend_back_second(
        lengths, packed, mixed, totals, grad_heads, done, grad_query
    )
    grad_packed = grad_packed.reshape(groups, row_count, span)
    pieces = [row_major(at_group(grad_packed, here ^ step)) for step in range(groups)]
    for one in late:
        one.piece = after(one.piece, pieces)
    sent = [one.send() for one in late]
    for one in late:
        one.receive()
    pieces = after(swap_pieces(pieces), sent)
    grad_projected = in_order(pieces)
    grad_down, grad_up, grad_out = [one.finish() for one in late]
    outcome = middle + live * (contract(hidden, full_down, ((1,), (0,))) + table[12])

    grad_qkv = [
        row_major(contract(normed_a, grad_projected[g], ((0,), (0,))).astype(bf16))
        for g in range(groups)
    ]
    sums = jnp.sum(grad_projected.astype(f32), axis=1)
    column_sums = by_kind([sums[g : g + 1] for g in range(groups)])[0]
    grad_norma = sum(
        contract(grad_projected[g], full_qkv[g], ((1,), (1,))) for g in range(groups)
    )
    start_part, gain_grad_a, shift_grad_a = norm_back(start, table[5], grad_norma)
    grad_start = grad_middle + start_part
    grad_embed = [
        jnp.sum(jnp.where(pass_of[:, index : index + 1], grad_start, 0.0), axis=0)
        for index in range(PASSES)
    ]
    vector_grads = jnp.stack(
        grad_embed
        + [
            gain_grad_a,
            shift_grad_a,
            column_sums[:width],
            column_sums[2 * width :],
            jnp.sum(grad_attn.astype(f32), axis=0),
            gain_grad_b,
            shift_grad_b,
            jnp.sum(grad_branch.astype(f32), axis=0),
        ]
    )
    bias_grads = jnp.sum(grad_upsum.astype(f32), axis=0)
    extra = [vector_grads.T.astype(bf16), bias_grads.reshape(width, ratio).astype(bf16)]
    extra = extra + [jnp.zeros((width, -small % 128), bf16)]
    sums_qkv = [
        Scatter(jnp.concatenate(grad_qkv[:half] + extra, axis=1), False).finish().astype(f32),
        Scatter(jnp.concatenate(grad_qkv[half:], axis=1), True).finish().astype(f32),
    ]
    extra = sums_qkv[0][:, half * span :]
    sums_qkv = [part[:, g * span : (g + 1) * span] for part in sums_qkv for g in range(half)]
    return (
        outcome.astype(bf16)[None],
        grad_start.astype(bf16)[None],
        by_kind(sums_qkv),
        grad_out.astype(f32),
        grad_up.astype(f32),
        grad_down.astype(f32),
        extra[:, :vector_count].T,
        extra[:, vector_count:small].reshape(own * ratio),
    )


def solution(mesh):
    split = P(both, None)
    return jax.shard_map(
        on_device,
        mesh=mesh,
        in_specs=(
            P("seq", "blk", None),
            P("seq", "blk", None),
            P("seq", None),
            split,
            split,
            split,
            split,
            P(None, both),
            P(both),
        ),
        out_specs=(
            P("seq", "blk", None),
            P("seq", "blk", None),
            split,
            split,
            split,
            split,
            P(None, both),
            P(both),
        ),
        check_vma=False,
    )
```

```python
import functools

import jax
import jax.numpy as jnp
from jax import lax
from jax.experimental import pallas as pl
from jax.experimental.layout import Layout, with_layout_constraint
from jax.experimental.pallas import tpu as pltpu
from jax.sharding import PartitionSpec as P

HEAD = 64
PASSES = 5
PASS_SLOTS = 512

masked_value = -1e30
both = ("seq", "blk")
f32 = jnp.float32
bf16 = jnp.bfloat16


def layer_norm(values, gain, offset):
    centre = values - jnp.mean(values, axis=-1, keepdims=True)
    spread = jnp.mean(centre * centre, axis=-1, keepdims=True)
    return centre * lax.rsqrt(spread + 1e-05) * gain + offset


def gelu_tanh(values):
    return jax.nn.gelu(values, approximate=True)


def contract(left, right, dims):
    return lax.dot_general(left, right, (dims, ((), ())), preferred_element_type=f32)


def tile_visible(length):
    key_place = lax.broadcasted_iota(jnp.int32, (PASS_SLOTS, PASS_SLOTS), 0)
    query_place = lax.broadcasted_iota(jnp.int32, (PASS_SLOTS, PASS_SLOTS), 1)
    return (key_place <= query_place) & (key_place < length)


def place_pieces(here, pieces, shelf, whole):
    span = pieces[0].shape[1]
    for step, piece in enumerate(pieces):
        shelf[here ^ step] = piece[...]
    for at in range(len(pieces)):
        whole[:, at * span : (at + 1) * span] = shelf[at]


def hand_out(here, whole, shelf, pieces):
    span = pieces[0].shape[1]
    for at in range(len(pieces)):
        shelf[at] = whole[:, at * span : (at + 1) * span]
    for step, piece in enumerate(pieces):
        piece[...] = shelf[here ^ step]


def turned(rows):
    return rows.astype(f32).T.astype(bf16)


def forward_kernel(groups, lengths, here, *refs):
    pieces, refs = refs[:groups], refs[groups:]
    packed, mixed, totals = refs[:3]
    outs, refs = refs[3 : 3 + groups], refs[3 + groups :]
    shelf, out_shelf, key_rows = refs
    place_pieces(here[0], pieces, shelf, packed)
    key_rows[...] = turned(packed[HEAD : 2 * HEAD, :])
    for query_index in range(PASSES):
        query_span = slice(query_index * PASS_SLOTS, (query_index + 1) * PASS_SLOTS)
        queries = packed[:HEAD, query_span] * jnp.asarray(0.125, bf16)
        top = jnp.full((1, PASS_SLOTS), masked_value, f32)
        total = jnp.zeros((1, PASS_SLOTS), f32)
        acc = jnp.zeros((HEAD, PASS_SLOTS), f32)
        for key_index in range(query_index + 1):
            key_span = slice(key_index * PASS_SLOTS, (key_index + 1) * PASS_SLOTS)
            scores = contract(key_rows[key_span, :], queries, ((1,), (0,)))
            scores = jnp.where(tile_visible(lengths[0, key_index]), scores, masked_value)
            newest = jnp.maximum(top, jnp.max(scores, axis=0, keepdims=True))
            shares = jnp.exp(scores - newest)
            fade = jnp.exp(top - newest)
            total = total * fade + jnp.sum(shares, axis=0, keepdims=True)
            values = packed[2 * HEAD :, key_span]
            acc = acc * fade + contract(values, shares.astype(bf16), ((1,), (0,)))
            top = newest
        mixed[:, query_span] = (acc / total).astype(bf16)
        totals[query_index : query_index + 1, :] = top + jnp.log(total)
    hand_out(here[0], mixed, out_shelf, outs)


def backward_kernel(groups, lengths, here, packed, mixed, totals, *refs):
    pieces, refs = refs[:groups], refs[groups:]
    outs, refs = refs[:groups], refs[groups:]
    shelf, out_shelf, grad, rows, grad_rows, grad_query, result = refs
    place_pieces(here[0], pieces, shelf, grad)
    rows[...] = turned(packed[...])
    grad_rows[...] = turned(grad[...])
    grad_query[...] = jnp.zeros_like(grad_query)
    eighth = jnp.asarray(0.125, bf16)

    def key_pass(key_index, _):
        key_at = pl.multiple_of(key_index * PASS_SLOTS, PASS_SLOTS)
        key_span = pl.ds(key_at, PASS_SLOTS)
        keys = rows[key_span, HEAD : 2 * HEAD] * eighth
        keys_turned = packed[HEAD : 2 * HEAD, key_span] * eighth
        values = rows[key_span, 2 * HEAD :]
        shown = tile_visible(lengths[0, key_index])

        def query_pass(query_index, carried):
            grad_key, grad_value = carried
            query_at = pl.multiple_of(query_index * PASS_SLOTS, PASS_SLOTS)
            query_span = pl.ds(query_at, PASS_SLOTS)
            grads = grad[:, query_span]
            product = grads.astype(f32) * mixed[:, query_span].astype(f32)
            delta = jnp.sum(product, axis=0, keepdims=True)
            scores = contract(keys, packed[:HEAD, query_span], ((1,), (0,)))
            shares = jnp.exp(scores - totals[pl.ds(query_index, 1), :])
            shares = jnp.where(shown, shares, 0.0)
            grad_shares = contract(values, grads, ((1,), (0,)))
            grad_scores = (shares * (grad_shares - delta)).astype(bf16)
            grad_query[:, query_span] += contract(keys_turned, grad_scores, ((1,), (0,)))
            grad_value += contract(shares.astype(bf16), grad_rows[query_span, :], ((1,), (0,)))
            queries = rows[query_span, :HEAD] * eighth
            grad_key += contract(grad_scores, queries, ((1,), (0,)))
            return grad_key, grad_value

        empty = jnp.zeros((PASS_SLOTS, HEAD), f32)
        grad_key, grad_value = lax.fori_loop(key_index, PASSES, query_pass, (empty, empty))
        result[HEAD : 2 * HEAD, key_span] = grad_key.T.astype(bf16)
        result[2 * HEAD :, key_span] = grad_value.T.astype(bf16)
        return 0

    lax.fori_loop(0, PASSES, key_pass, 0)
    result[:HEAD, :] = grad_query[...].astype(bf16)
    hand_out(here[0], result, out_shelf, outs)


in_vmem = functools.partial(pl.BlockSpec, memory_space=pltpu.VMEM)
in_smem = functools.partial(pl.BlockSpec, memory_space=pltpu.SMEM)


def attend(lengths, here, pieces):
    groups = len(pieces)
    triple, span = pieces[0].shape
    slots = span * groups
    return pl.pallas_call(
        functools.partial(forward_kernel, groups),
        out_shape=[
            jax.ShapeDtypeStruct((triple, slots), bf16),
            jax.ShapeDtypeStruct((HEAD, slots), bf16),
            jax.ShapeDtypeStruct((PASSES, PASS_SLOTS), f32),
        ]
        + [jax.ShapeDtypeStruct((HEAD, span), bf16)] * groups,
        in_specs=[in_smem(), in_smem()] + [in_vmem()] * groups,
        out_specs=[in_vmem()] * (3 + groups),
        scratch_shapes=[
            pltpu.VMEM((groups, triple, span), bf16),
            pltpu.VMEM((groups, HEAD, span), bf16),
            pltpu.VMEM((slots, HEAD), bf16),
        ],
        compiler_params=pltpu.CompilerParams(vmem_limit_bytes=32 << 20),
        cost_estimate=pl.CostEstimate(flops=10**10, transcendentals=0, bytes_accessed=10**6),
        name="attend",
    )(lengths, here, *pieces)


def attend_back(lengths, here, packed, mixed, totals, pieces):
    groups = len(pieces)
    triple, slots = packed.shape
    span = slots // groups
    return pl.pallas_call(
        functools.partial(backward_kernel, groups),
        out_shape=[jax.ShapeDtypeStruct((triple, span), bf16)] * groups,
        in_specs=[in_smem(), in_smem()] + [in_vmem()] * (3 + groups),
        out_specs=[in_vmem()] * groups,
        scratch_shapes=[
            pltpu.VMEM((groups, HEAD, span), bf16),
            pltpu.VMEM((groups, triple, span), bf16),
            pltpu.VMEM((HEAD, slots), bf16),
            pltpu.VMEM((slots, triple), bf16),
            pltpu.VMEM((slots, HEAD), bf16),
            pltpu.VMEM((HEAD, slots), f32),
            pltpu.VMEM((triple, slots), bf16),
        ],
        compiler_params=pltpu.CompilerParams(vmem_limit_bytes=32 << 20),
        cost_estimate=pl.CostEstimate(
            flops=15 * 10**9, transcendentals=0, bytes_accessed=10**6
        ),
        name="attend_back",
    )(lengths, here, packed, mixed, totals, *pieces)


def row_major(values):
    return with_layout_constraint(values, Layout(tuple(range(values.ndim))))


def after(values, *others):
    return lax.optimization_barrier((values, others))[0]


def swap_with(values, axis, step):
    size = lax.axis_size(axis)
    return lax.ppermute(values, axis, [(i, i ^ step) for i in range(size)])


def axis_bits(axis):
    size = lax.axis_size(axis)
    assert size & (size - 1) == 0
    return [(axis, 1 << n) for n in reversed(range(size.bit_length() - 1))]


def bit_order(flip):
    places = axis_bits("seq") + axis_bits("blk")
    near = axis_bits("seq")
    far = near[:-1][::-1] if flip else near[:-1]
    return places, axis_bits("blk") + far + near[-1:]


def own_bit(bit):
    return (lax.axis_index(bit[0]) & bit[1]) != 0


class Gather:
    def __init__(self, piece, flip):
        self.places, self.order = bit_order(flip)
        self.shape = piece.shape
        self.piece = piece
        self.done = []

    def grow(self, count=None):
        count = len(self.order) if count is None else count
        for bit in self.order[:count]:
            other = swap_with(self.piece, *bit)
            self.done = sorted(self.done + [bit], key=self.places.index)
            mine = own_bit(bit)
            low = jnp.where(mine, other, self.piece)
            high = jnp.where(mine, self.piece, other)
            self.piece = jnp.stack([low, high], axis=self.done.index(bit))
        self.order = self.order[count:]
        return self.piece

    def whole(self):
        return self.grow().reshape((-1,) + self.shape[1:])


class Scatter:
    def __init__(self, whole, flip):
        self.left, order = bit_order(flip)
        self.order = order[::-1]
        rows = whole.shape[0] >> len(order)
        self.piece = whole.reshape((2,) * len(order) + (rows,) + whole.shape[1:])

    def send(self):
        bit, self.order = self.order[0], self.order[1:]
        at = self.left.index(bit)
        self.left = [place for place in self.left if place != bit]
        low = lax.index_in_dim(self.piece, 0, at, keepdims=False)
        high = lax.index_in_dim(self.piece, 1, at, keepdims=False)
        mine = own_bit(bit)
        self.bit = bit
        self.sent = jnp.where(mine, low, high)
        self.kept = jnp.where(mine, high, low)
        return (self.sent, self.kept)

    def receive(self):
        other = swap_with(self.sent, *self.bit)
        self.piece = (self.kept.astype(f32) + other.astype(f32)).astype(bf16)

    def finish(self):
        while self.order:
            self.send()
            self.receive()
        return self.piece


def swap_pieces(pieces):
    return [swap_with(piece, "blk", step) if step else piece for step, piece in enumerate(pieces)]


def in_order(pieces):
    here = lax.axis_index("blk")
    result = jnp.zeros((len(pieces),) + pieces[0].shape, pieces[0].dtype)
    for step, piece in enumerate(pieces):
        result = lax.dynamic_update_index_in_dim(result, piece, here ^ step, 0)
    return result


def at_group(values, group):
    return lax.dynamic_index_in_dim(values, group, 0, keepdims=False)


def by_head(rows, groups):
    count = rows.shape[0]
    return rows.reshape(count, 3, groups, -1, HEAD).transpose(0, 3, 2, 1, 4).reshape(count, -1)


def by_kind(rows, groups):
    count = rows.shape[0]
    return rows.reshape(count, -1, groups, 3, HEAD).transpose(0, 3, 2, 1, 4).reshape(count, -1)


def norm_parts(values):
    centre = values - jnp.mean(values, axis=-1, keepdims=True)
    spread = jnp.mean(centre * centre, axis=-1, keepdims=True)
    scale = lax.rsqrt(spread + 1e-05)
    return centre * scale, scale


def norm_back(values, gain, grad):
    hat, scale = norm_parts(values)
    edge = grad * gain
    part = scale * (
        edge
        - jnp.mean(edge, axis=-1, keepdims=True)
        - hat * jnp.mean(edge * hat, axis=-1, keepdims=True)
    )
    return part, jnp.sum(grad * hat, axis=0), jnp.sum(grad, axis=0)


def on_device(states, cotangent, lengths, w_qkv, w_out, w_up, w_down, vectors, up_bias):
    _, row_count, width = states.shape
    groups = lax.axis_size("blk")
    own = w_qkv.shape[0]
    wide = w_up.shape[1]
    ratio = wide // width
    vector_count = vectors.shape[0]
    heads = width // HEAD // groups
    span = 3 * HEAD
    small = vector_count + ratio

    here = lax.axis_index("blk").astype(jnp.int32)
    parts = by_head(w_qkv, groups)
    middle_column = parts.shape[1] // 2
    extra = [vectors.T, up_bias.reshape(own, ratio), jnp.zeros((own, -small % 128), bf16)]
    streams = [
        Gather(jnp.concatenate([parts[:, :middle_column]] + extra, axis=1), False),
        Gather(parts[:, middle_column:], True),
    ]
    blk_steps = len(axis_bits("blk"))
    begun = [stream.grow(blk_steps) for stream in streams]
    w_out, w_up, w_down = after((w_out, w_up, w_down), begun)
    later = [Gather(w_up, False), Gather(w_down, True), Gather(w_out, False)]
    for one in later:
        one.grow(blk_steps)
    first = [stream.whole() for stream in streams]
    for one in later:
        one.piece = after(one.piece, first)
        one.grow(1)
    full_qkv = jnp.concatenate([first[0][:, :middle_column], first[1]], axis=1)
    head_qkv = [full_qkv[:, h * groups * span : (h + 1) * groups * span] for h in range(heads)]
    corner = first[0][:, middle_column : middle_column + small]
    table = corner[:, :vector_count].astype(f32).T
    bias_up = corner[:, vector_count:].astype(f32).reshape(wide)

    slots = lax.axis_index("blk") * row_count + jnp.arange(row_count, dtype=jnp.int32)
    pass_of = (slots // PASS_SLOTS)[:, None] == jnp.arange(PASSES, dtype=jnp.int32)[None, :]
    bounds = jnp.sum(jnp.where(pass_of, lengths[0][None, :], 0), axis=1)
    live = (slots % PASS_SLOTS < bounds).astype(f32)[:, None]

    added = jnp.zeros((row_count, width), f32)
    for index in range(PASSES):
        added = jnp.where(pass_of[:, index : index + 1], table[index], added)
    start = states[0].astype(f32) + added
    normed_a = layer_norm(start, table[5], table[6]).astype(bf16)
    bias_three = jnp.concatenate([table[7], jnp.zeros_like(table[7]), table[8]])
    bias_three = by_head(bias_three[None], groups).reshape(heads, -1, 1)
    sending = []
    for h in range(heads):
        rows = contract(head_qkv[h], normed_a, ((0,), (1,))) + bias_three[h]
        rows = rows.astype(bf16).reshape(groups, span, row_count)
        sending.append([row_major(at_group(rows, here ^ step)) for step in range(groups)])
    for one in later:
        one.piece = after(one.piece, sending)
    kept = []
    arrived = []
    returned = []
    for h in range(heads):
        pieces = swap_pieces(after(sending[h], arrived))
        arrived = pieces
        packed, mixed, totals, *pieces = attend(lengths, here[None], pieces)
        kept.append((packed, mixed, totals))
        returned.append(in_order(swap_pieces(pieces)))
    full_up, full_down, full_out = [one.whole() for one in later]
    heads_out = jnp.stack(returned, axis=1).reshape(width, row_count)
    middle = start + live * (contract(heads_out, full_out, ((0,), (0,))) + table[9])
    normed_b = layer_norm(middle, table[10], table[11]).astype(bf16)
    up_sum = contract(normed_b, full_up, ((1,), (0,))) + bias_up
    activated, gelu_pull = jax.vjp(gelu_tanh, up_sum)
    hidden = activated.astype(bf16)
    incoming = cotangent[0].astype(f32)
    grad_branch = (live * incoming).astype(bf16)
    grad_hidden = contract(grad_branch, full_down, ((1,), (1,)))
    grad_upsum = gelu_pull(grad_hidden)[0].astype(bf16)
    grad_normb = contract(grad_upsum, full_up, ((1,), (1,)))
    middle_part, gain_grad_b, shift_grad_b = norm_back(middle, table[10], grad_normb)
    grad_middle = incoming + middle_part
    grad_attn = (live * grad_middle).astype(bf16)
    grad_heads = contract(full_out, grad_attn, ((1,), (1,))).astype(bf16)
    grad_heads = grad_heads.reshape(groups, heads, HEAD, row_count)
    sending = [
        [row_major(at_group(grad_heads[:, h], here ^ step)) for step in range(groups)]
        for h in range(heads)
    ]
    arrived = []
    late = []
    parts = []
    for h in range(heads):
        pieces = swap_pieces(after(sending[h], arrived))
        arrived = pieces
        if late:
            for one in late:
                one.piece = after(one.piece, parts[-1])
            sent = [one.send() for one in late]
            for one in late:
                one.receive()
            pieces = after(pieces, sent)
        back = attend_back(lengths, here[None], *kept[h], pieces)
        if not late:
            hidden_late, grad_branch_late, grad_upsum_late, grad_attn_late = after(
                (hidden, grad_branch, grad_upsum, grad_attn), back
            )
            grad_down = contract(hidden_late, grad_branch_late, ((0,), (0,))).astype(bf16)
            grad_up = contract(normed_b, grad_upsum_late, ((0,), (0,))).astype(bf16)
            grad_out = contract(heads_out, grad_attn_late, ((1,), (0,))).astype(bf16)
            late = [Scatter(grad_down, True), Scatter(grad_up, False), Scatter(grad_out, False)]
        parts.append(back)
    grad_projected = [in_order(swap_pieces(back)) for back in parts]
    for one in late:
        one.piece = after(one.piece, parts[-1])
    grad_down, grad_up, grad_out = [one.finish() for one in late]
    outcome = middle + live * (contract(hidden, full_down, ((1,), (0,))) + table[12])

    grad_projected = [part.reshape(groups * span, row_count) for part in grad_projected]
    grad_qkv = [
        row_major(contract(normed_a, part, ((0,), (1,))).astype(bf16)) for part in grad_projected
    ]
    grad_qkv = [Scatter(part, h % 2 == 1).finish() for h, part in enumerate(grad_qkv)]
    sums = [jnp.sum(part.astype(f32), axis=1) for part in grad_projected]
    column_sums = by_kind(jnp.concatenate(sums)[None], groups)[0]
    grad_norma = sum(
        contract(part, weights, ((0,), (1,))) for part, weights in zip(grad_projected, head_qkv)
    )
    start_part, gain_grad_a, shift_grad_a = norm_back(start, table[5], grad_norma)
    grad_start = grad_middle + start_part
    grad_embed = [
        jnp.sum(jnp.where(pass_of[:, index : index + 1], grad_start, 0.0), axis=0)
        for index in range(PASSES)
    ]
    vector_grads = jnp.stack(
        grad_embed
        + [
            gain_grad_a,
            shift_grad_a,
            column_sums[:width],
            column_sums[2 * width :],
            jnp.sum(grad_attn.astype(f32), axis=0),
            gain_grad_b,
            shift_grad_b,
            jnp.sum(grad_branch.astype(f32), axis=0),
        ]
    )
    bias_grads = jnp.sum(grad_upsum.astype(f32), axis=0)
    extra = [vector_grads.T.astype(bf16), bias_grads.reshape(width, ratio).astype(bf16)]
    extra = jnp.concatenate(extra + [jnp.zeros((width, -small % 128), bf16)], axis=1)
    extra = Scatter(extra, False).finish().astype(f32)
    return (
        outcome.astype(bf16)[None],
        grad_start.astype(bf16)[None],
        by_kind(jnp.concatenate(grad_qkv, axis=1).astype(f32), groups),
        grad_out.astype(f32),
        grad_up.astype(f32),
        grad_down.astype(f32),
        extra[:, :vector_count].T,
        extra[:, vector_count:small].reshape(own * ratio),
    )


def solution(mesh):
    split = P(both, None)
    return jax.shard_map(
        on_device,
        mesh=mesh,
        in_specs=(
            P("seq", "blk", None),
            P("seq", "blk", None),
            P("seq", None),
            split,
            split,
            split,
            split,
            P(None, both),
            P(both),
        ),
        out_specs=(
            P("seq", "blk", None),
            P("seq", "blk", None),
            split,
            split,
            split,
            split,
            P(None, both),
            P(both),
        ),
        check_vma=False,
    )
```

```python
import functools

import jax
import jax.numpy as jnp
from jax import lax
from jax.experimental import pallas as pl
from jax.experimental.layout import Layout, with_layout_constraint
from jax.experimental.pallas import tpu as pltpu
from jax.sharding import PartitionSpec as P

HEAD = 64
PASSES = 5
PASS_SLOTS = 512


masked_value = -1e30
both = ("seq", "blk")
f32 = jnp.float32
bf16 = jnp.bfloat16


def layer_norm(values, gain, offset):
    centre = values - jnp.mean(values, axis=-1, keepdims=True)
    spread = jnp.mean(centre * centre, axis=-1, keepdims=True)
    return centre * lax.rsqrt(spread + 1e-05) * gain + offset


def gelu_tanh(values):
    return jax.nn.gelu(values, approximate=True)


def contract(left, right, dims):
    return lax.dot_general(left, right, (dims, ((), ())), preferred_element_type=f32)


def tile_visible(length):
    key_place = lax.broadcasted_iota(jnp.int32, (PASS_SLOTS, PASS_SLOTS), 0)
    query_place = lax.broadcasted_iota(jnp.int32, (PASS_SLOTS, PASS_SLOTS), 1)
    return (key_place <= query_place) & (key_place < length)


def place_pieces(here, pieces, shelf, whole):
    span = pieces[0].shape[1]
    for step, piece in enumerate(pieces):
        shelf[here ^ step] = piece[...]
    for at in range(len(pieces)):
        whole[:, at * span : (at + 1) * span] = shelf[at]


def hand_out(here, whole, shelf, pieces):
    span = pieces[0].shape[1]
    for at in range(len(pieces)):
        shelf[at] = whole[:, at * span : (at + 1) * span]
    for step, piece in enumerate(pieces):
        piece[...] = shelf[here ^ step]


def turned(rows):
    return rows.astype(f32).T.astype(bf16)


def forward_kernel(groups, lengths, here, *refs):
    pieces, refs = refs[:groups], refs[groups:]
    packed, mixed, totals = refs[:3]
    outs, refs = refs[3 : 3 + groups], refs[3 + groups :]
    shelf, out_shelf, key_rows = refs
    place_pieces(here[0], pieces, shelf, packed)
    key_rows[...] = turned(packed[HEAD : 2 * HEAD, :])
    for query_index in range(PASSES):
        query_span = slice(query_index * PASS_SLOTS, (query_index + 1) * PASS_SLOTS)
        queries = packed[:HEAD, query_span] * jnp.asarray(0.125, bf16)
        top = jnp.full((1, PASS_SLOTS), masked_value, f32)
        total = jnp.zeros((1, PASS_SLOTS), f32)
        acc = jnp.zeros((HEAD, PASS_SLOTS), f32)
        for key_index in range(query_index + 1):
            key_span = slice(key_index * PASS_SLOTS, (key_index + 1) * PASS_SLOTS)
            scores = contract(key_rows[key_span, :], queries, ((1,), (0,)))
            scores = jnp.where(tile_visible(lengths[0, key_index]), scores, masked_value)
            newest = jnp.maximum(top, jnp.max(scores, axis=0, keepdims=True))
            shares = jnp.exp(scores - newest)
            fade = jnp.exp(top - newest)
            total = total * fade + jnp.sum(shares, axis=0, keepdims=True)
            values = packed[2 * HEAD :, key_span]
            acc = acc * fade + contract(values, shares.astype(bf16), ((1,), (0,)))
            top = newest
        mixed[:, query_span] = (acc / total).astype(bf16)
        totals[query_index : query_index + 1, :] = top + jnp.log(total)
    hand_out(here[0], mixed, out_shelf, outs)


def backward_kernel(groups, lengths, here, packed, mixed, totals, *refs):
    pieces, refs = refs[:groups], refs[groups:]
    outs, refs = refs[:groups], refs[groups:]
    shelf, out_shelf, grad, rows, grad_rows, grad_query, result = refs
    place_pieces(here[0], pieces, shelf, grad)
    rows[...] = turned(packed[...])
    grad_rows[...] = turned(grad[...])
    grad_query[...] = jnp.zeros_like(grad_query)
    eighth = jnp.asarray(0.125, bf16)

    def key_pass(key_index, _):
        key_at = pl.multiple_of(key_index * PASS_SLOTS, PASS_SLOTS)
        key_span = pl.ds(key_at, PASS_SLOTS)
        keys = rows[key_span, HEAD : 2 * HEAD] * eighth
        keys_turned = packed[HEAD : 2 * HEAD, key_span] * eighth
        values = rows[key_span, 2 * HEAD :]
        shown = tile_visible(lengths[0, key_index])

        def query_pass(query_index, carried):
            grad_key, grad_value = carried
            query_at = pl.multiple_of(query_index * PASS_SLOTS, PASS_SLOTS)
            query_span = pl.ds(query_at, PASS_SLOTS)
            grads = grad[:, query_span]
            product = grads.astype(f32) * mixed[:, query_span].astype(f32)
            delta = jnp.sum(product, axis=0, keepdims=True)
            scores = contract(keys, packed[:HEAD, query_span], ((1,), (0,)))
            shares = jnp.exp(scores - totals[pl.ds(query_index, 1), :])
            shares = jnp.where(shown, shares, 0.0)
            grad_shares = contract(values, grads, ((1,), (0,)))
            grad_scores = (shares * (grad_shares - delta)).astype(bf16)
            grad_query[:, query_span] += contract(keys_turned, grad_scores, ((1,), (0,)))
            grad_value += contract(shares.astype(bf16), grad_rows[query_span, :], ((1,), (0,)))
            queries = rows[query_span, :HEAD] * eighth
            grad_key += contract(grad_scores, queries, ((1,), (0,)))
            return grad_key, grad_value

        empty = jnp.zeros((PASS_SLOTS, HEAD), f32)
        grad_key, grad_value = lax.fori_loop(key_index, PASSES, query_pass, (empty, empty))
        result[HEAD : 2 * HEAD, key_span] = grad_key.T.astype(bf16)
        result[2 * HEAD :, key_span] = grad_value.T.astype(bf16)
        return 0

    lax.fori_loop(0, PASSES, key_pass, 0)
    result[:HEAD, :] = grad_query[...].astype(bf16)
    hand_out(here[0], result, out_shelf, outs)


in_vmem = functools.partial(pl.BlockSpec, memory_space=pltpu.VMEM)
in_smem = functools.partial(pl.BlockSpec, memory_space=pltpu.SMEM)


def attend(lengths, here, pieces):
    groups = len(pieces)
    triple, span = pieces[0].shape
    slots = span * groups
    return pl.pallas_call(
        functools.partial(forward_kernel, groups),
        out_shape=[
            jax.ShapeDtypeStruct((triple, slots), bf16),
            jax.ShapeDtypeStruct((HEAD, slots), bf16),
            jax.ShapeDtypeStruct((PASSES, PASS_SLOTS), f32),
        ]
        + [jax.ShapeDtypeStruct((HEAD, span), bf16)] * groups,
        in_specs=[in_smem(), in_smem()] + [in_vmem()] * groups,
        out_specs=[in_vmem()] * (3 + groups),
        scratch_shapes=[
            pltpu.VMEM((groups, triple, span), bf16),
            pltpu.VMEM((groups, HEAD, span), bf16),
            pltpu.VMEM((slots, HEAD), bf16),
        ],
        compiler_params=pltpu.CompilerParams(vmem_limit_bytes=32 << 20),
        cost_estimate=pl.CostEstimate(flops=10**10, transcendentals=0, bytes_accessed=10**6),
        name="attend",
    )(lengths, here, *pieces)


def attend_back(lengths, here, packed, mixed, totals, pieces):
    groups = len(pieces)
    triple, slots = packed.shape
    span = slots // groups
    return pl.pallas_call(
        functools.partial(backward_kernel, groups),
        out_shape=[jax.ShapeDtypeStruct((triple, span), bf16)] * groups,
        in_specs=[in_smem(), in_smem()] + [in_vmem()] * (3 + groups),
        out_specs=[in_vmem()] * groups,
        scratch_shapes=[
            pltpu.VMEM((groups, HEAD, span), bf16),
            pltpu.VMEM((groups, triple, span), bf16),
            pltpu.VMEM((HEAD, slots), bf16),
            pltpu.VMEM((slots, triple), bf16),
            pltpu.VMEM((slots, HEAD), bf16),
            pltpu.VMEM((HEAD, slots), f32),
            pltpu.VMEM((triple, slots), bf16),
        ],
        compiler_params=pltpu.CompilerParams(vmem_limit_bytes=32 << 20),
        cost_estimate=pl.CostEstimate(
            flops=15 * 10**9, transcendentals=0, bytes_accessed=10**6
        ),
        name="attend_back",
    )(lengths, here, packed, mixed, totals, *pieces)


def row_major(values):
    return with_layout_constraint(values, Layout(tuple(range(values.ndim))))


def after(values, *others):
    return lax.optimization_barrier((values, others))[0]


def swap_with(values, axis, step):
    size = lax.axis_size(axis)
    return lax.ppermute(values, axis, [(i, i ^ step) for i in range(size)])


def axis_bits(axis):
    size = lax.axis_size(axis)
    assert size & (size - 1) == 0
    return [(axis, 1 << n) for n in reversed(range(size.bit_length() - 1))]


def bit_order(flip):
    places = axis_bits("seq") + axis_bits("blk")
    near = axis_bits("seq")
    far = near[:-1][::-1] if flip else near[:-1]
    return places, axis_bits("blk") + far + near[-1:]


def own_bit(bit):
    return (lax.axis_index(bit[0]) & bit[1]) != 0


class Gather:
    def __init__(self, piece, flip):
        self.places, self.order = bit_order(flip)
        self.shape = piece.shape
        self.piece = piece
        self.done = []

    def grow(self, count=None):
        count = len(self.order) if count is None else count
        for bit in self.order[:count]:
            other = swap_with(self.piece, *bit)
            self.done = sorted(self.done + [bit], key=self.places.index)
            mine = own_bit(bit)
            low = jnp.where(mine, other, self.piece)
            high = jnp.where(mine, self.piece, other)
            self.piece = jnp.stack([low, high], axis=self.done.index(bit))
        self.order = self.order[count:]
        return self.piece

    def whole(self):
        return self.grow().reshape((-1,) + self.shape[1:])


class Scatter:
    def __init__(self, whole, flip):
        self.left, order = bit_order(flip)
        self.order = order[::-1]
        rows = whole.shape[0] >> len(order)
        self.piece = whole.reshape((2,) * len(order) + (rows,) + whole.shape[1:])

    def send(self):
        bit, self.order = self.order[0], self.order[1:]
        at = self.left.index(bit)
        self.left = [place for place in self.left if place != bit]
        low = lax.index_in_dim(self.piece, 0, at, keepdims=False)
        high = lax.index_in_dim(self.piece, 1, at, keepdims=False)
        mine = own_bit(bit)
        self.bit = bit
        self.sent = jnp.where(mine, low, high)
        self.kept = jnp.where(mine, high, low)
        return (self.sent, self.kept)

    def receive(self, *others):
        other = after(swap_with(self.sent, *self.bit), others)
        self.piece = (self.kept.astype(f32) + other.astype(f32)).astype(bf16)

    def finish(self):
        while self.order:
            self.send()
            self.receive()
        return self.piece


def swap_pieces(pieces):
    return [swap_with(piece, "blk", step) if step else piece for step, piece in enumerate(pieces)]


def in_order(pieces):
    here = lax.axis_index("blk")
    result = jnp.zeros((len(pieces),) + pieces[0].shape, pieces[0].dtype)
    for step, piece in enumerate(pieces):
        result = lax.dynamic_update_index_in_dim(result, piece, here ^ step, 0)
    return result


def at_group(values, group):
    return lax.dynamic_index_in_dim(values, group, 0, keepdims=False)


def by_head(rows, groups):
    count = rows.shape[0]
    return rows.reshape(count, 3, groups, -1, HEAD).transpose(0, 3, 2, 1, 4).reshape(count, -1)


def by_kind(rows, groups):
    count = rows.shape[0]
    return rows.reshape(count, -1, groups, 3, HEAD).transpose(0, 3, 2, 1, 4).reshape(count, -1)


def norm_parts(values):
    centre = values - jnp.mean(values, axis=-1, keepdims=True)
    spread = jnp.mean(centre * centre, axis=-1, keepdims=True)
    scale = lax.rsqrt(spread + 1e-05)
    return centre * scale, scale


def norm_back(values, gain, grad):
    hat, scale = norm_parts(values)
    edge = grad * gain
    part = scale * (
        edge
        - jnp.mean(edge, axis=-1, keepdims=True)
        - hat * jnp.mean(edge * hat, axis=-1, keepdims=True)
    )
    return part, jnp.sum(grad * hat, axis=0), jnp.sum(grad, axis=0)


def on_device(states, cotangent, lengths, w_qkv, w_out, w_up, w_down, vectors, up_bias):
    _, row_count, width = states.shape
    groups = lax.axis_size("blk")
    own = w_qkv.shape[0]
    wide = w_up.shape[1]
    ratio = wide // width
    vector_count = vectors.shape[0]
    heads = width // HEAD // groups
    span = 3 * HEAD
    small = vector_count + ratio

    here = lax.axis_index("blk").astype(jnp.int32)
    parts = by_head(w_qkv, groups)
    middle_column = parts.shape[1] // 2
    extra = [vectors.T, up_bias.reshape(own, ratio), jnp.zeros((own, -small % 128), bf16)]
    streams = [
        Gather(jnp.concatenate([parts[:, :middle_column]] + extra, axis=1), False),
        Gather(parts[:, middle_column:], True),
    ]
    blk_steps = len(axis_bits("blk"))
    begun = [stream.grow(blk_steps) for stream in streams]
    w_out, w_up, w_down = after((w_out, w_up, w_down), begun)
    later = [Gather(w_up, False), Gather(w_down, True), Gather(w_out, False)]
    for one in later:
        one.grow(blk_steps)
    first = [stream.whole() for stream in streams]
    for one in later:
        one.piece = after(one.piece, first)
        one.grow(1)
    full_qkv = jnp.concatenate([first[0][:, :middle_column], first[1]], axis=1)
    head_qkv = [full_qkv[:, h * groups * span : (h + 1) * groups * span] for h in range(heads)]
    corner = first[0][:, middle_column : middle_column + small]
    table = corner[:, :vector_count].astype(f32).T
    bias_up = corner[:, vector_count:].astype(f32).reshape(wide)

    slots = lax.axis_index("blk") * row_count + jnp.arange(row_count, dtype=jnp.int32)
    pass_of = (slots // PASS_SLOTS)[:, None] == jnp.arange(PASSES, dtype=jnp.int32)[None, :]
    bounds = jnp.sum(jnp.where(pass_of, lengths[0][None, :], 0), axis=1)
    live = (slots % PASS_SLOTS < bounds).astype(f32)[:, None]

    added = jnp.zeros((row_count, width), f32)
    for index in range(PASSES):
        added = jnp.where(pass_of[:, index : index + 1], table[index], added)
    start = states[0].astype(f32) + added
    normed_a = layer_norm(start, table[5], table[6]).astype(bf16)
    bias_three = jnp.concatenate([table[7], jnp.zeros_like(table[7]), table[8]])
    bias_three = by_head(bias_three[None], groups).reshape(heads, -1, 1)
    sending = []
    for h in range(heads):
        rows = contract(head_qkv[h], normed_a, ((0,), (1,))) + bias_three[h]
        rows = rows.astype(bf16).reshape(groups, span, row_count)
        sending.append([row_major(at_group(rows, here ^ step)) for step in range(groups)])
    for one in later:
        one.piece = after(one.piece, sending)
    kept = []
    arrived = []
    returned = []
    for h in range(heads):
        pieces = swap_pieces(after(sending[h], arrived))
        arrived = pieces
        packed, mixed, totals, *pieces = attend(lengths, here[None], pieces)
        kept.append((packed, mixed, totals))
        returned.append(swap_pieces(pieces))
    full_up, full_down, full_out = [one.whole() for one in later]
    returned[:-1] = after(returned[:-1], pieces)
    returned = [in_order(pieces) for pieces in returned]
    heads_out = jnp.stack(returned, axis=1).reshape(width, row_count)
    middle = start + live * (contract(heads_out, full_out, ((0,), (0,))) + table[9])
    normed_b = layer_norm(middle, table[10], table[11]).astype(bf16)
    up_sum = contract(normed_b, full_up, ((1,), (0,))) + bias_up
    activated, gelu_pull = jax.vjp(gelu_tanh, up_sum)
    hidden = activated.astype(bf16)
    incoming = cotangent[0].astype(f32)
    grad_branch = (live * incoming).astype(bf16)
    grad_hidden = contract(grad_branch, full_down, ((1,), (1,)))
    grad_upsum = gelu_pull(grad_hidden)[0].astype(bf16)
    grad_normb = contract(grad_upsum, full_up, ((1,), (1,)))
    middle_part, gain_grad_b, shift_grad_b = norm_back(middle, table[10], grad_normb)
    grad_middle = incoming + middle_part
    grad_attn = (live * grad_middle).astype(bf16)
    grad_heads = contract(full_out, grad_attn, ((1,), (1,))).astype(bf16)
    grad_heads = grad_heads.reshape(groups, heads, HEAD, row_count)
    sending = [
        [row_major(at_group(grad_heads[:, h], here ^ step)) for step in range(groups)]
        for h in range(heads)
    ]
    arrived = []
    late = []
    parts = []
    for h in range(heads):
        pieces = swap_pieces(after(sending[h], arrived))
        arrived = pieces
        if late:
            if h > 1:
                for one in late:
                    one.receive(parts[-1])
            pieces = after(pieces, [one.send() for one in late])
        back = attend_back(lengths, here[None], *kept[h], pieces)
        if not late:
            hidden_late, grad_branch_late, grad_upsum_late, grad_attn_late = after(
                (hidden, grad_branch, grad_upsum, grad_attn), back
            )
            grad_down = contract(hidden_late, grad_branch_late, ((0,), (0,))).astype(bf16)
            grad_up = contract(normed_b, grad_upsum_late, ((0,), (0,))).astype(bf16)
            grad_out = contract(heads_out, grad_attn_late, ((1,), (0,))).astype(bf16)
            late = [Scatter(grad_down, True), Scatter(grad_up, False), Scatter(grad_out, False)]
        parts.append(back)
    grad_projected = [swap_pieces(back) for back in parts]
    grad_projected[:-1] = after(grad_projected[:-1], parts[-1])
    grad_projected = [in_order(pieces) for pieces in grad_projected]
    for one in late:
        one.receive(parts[-1])
    grad_down, grad_up, grad_out = [one.finish() for one in late]
    outcome = middle + live * (contract(hidden, full_down, ((1,), (0,))) + table[12])

    grad_projected = [part.reshape(groups * span, row_count) for part in grad_projected]
    grad_qkv = [
        row_major(contract(normed_a, part, ((0,), (1,))).astype(bf16)) for part in grad_projected
    ]
    grad_qkv = [Scatter(part, h % 2 == 1).finish() for h, part in enumerate(grad_qkv)]
    sums = [jnp.sum(part.astype(f32), axis=1) for part in grad_projected]
    column_sums = by_kind(jnp.concatenate(sums)[None], groups)[0]
    grad_norma = sum(
        contract(part, weights, ((0,), (1,))) for part, weights in zip(grad_projected, head_qkv)
    )
    start_part, gain_grad_a, shift_grad_a = norm_back(start, table[5], grad_norma)
    grad_start = grad_middle + start_part
    grad_embed = [
        jnp.sum(jnp.where(pass_of[:, index : index + 1], grad_start, 0.0), axis=0)
        for index in range(PASSES)
    ]
    vector_grads = jnp.stack(
        grad_embed
        + [
            gain_grad_a,
            shift_grad_a,
            column_sums[:width],
            column_sums[2 * width :],
            jnp.sum(grad_attn.astype(f32), axis=0),
            gain_grad_b,
            shift_grad_b,
            jnp.sum(grad_branch.astype(f32), axis=0),
        ]
    )
    bias_grads = jnp.sum(grad_upsum.astype(f32), axis=0)
    extra = [vector_grads.T.astype(bf16), bias_grads.reshape(width, ratio).astype(bf16)]
    extra = jnp.concatenate(extra + [jnp.zeros((width, -small % 128), bf16)], axis=1)
    extra = Scatter(extra, False).finish().astype(f32)
    return (
        outcome.astype(bf16)[None],
        grad_start.astype(bf16)[None],
        by_kind(jnp.concatenate(grad_qkv, axis=1).astype(f32), groups),
        grad_out.astype(f32),
        grad_up.astype(f32),
        grad_down.astype(f32),
        extra[:, :vector_count].T,
        extra[:, vector_count:small].reshape(own * ratio),
    )


def solution(mesh):
    split = P(both, None)
    return jax.shard_map(
        on_device,
        mesh=mesh,
        in_specs=(
            P("seq", "blk", None),
            P("seq", "blk", None),
            P("seq", None),
            split,
            split,
            split,
            split,
            P(None, both),
            P(both),
        ),
        out_specs=(
            P("seq", "blk", None),
            P("seq", "blk", None),
            split,
            split,
            split,
            split,
            P(None, both),
            P(both),
        ),
        check_vma=False,
    )
```

```python
import functools

import jax
import jax.numpy as jnp
from jax import lax
from jax.experimental import pallas as pl
from jax.experimental.layout import Layout, with_layout_constraint
from jax.experimental.pallas import tpu as pltpu
from jax.sharding import PartitionSpec as P

HEAD = 64
PASSES = 5
PASS_SLOTS = 512


masked_value = -1e30
both = ("seq", "blk")
f32 = jnp.float32
bf16 = jnp.bfloat16


def layer_norm(values, gain, offset):
    centre = values - jnp.mean(values, axis=-1, keepdims=True)
    spread = jnp.mean(centre * centre, axis=-1, keepdims=True)
    return centre * lax.rsqrt(spread + 1e-05) * gain + offset


def gelu_tanh(values):
    return jax.nn.gelu(values, approximate=True)


def contract(left, right, dims):
    return lax.dot_general(left, right, (dims, ((), ())), preferred_element_type=f32)


def tile_visible(length):
    key_place = lax.broadcasted_iota(jnp.int32, (PASS_SLOTS, PASS_SLOTS), 0)
    query_place = lax.broadcasted_iota(jnp.int32, (PASS_SLOTS, PASS_SLOTS), 1)
    return (key_place <= query_place) & (key_place < length)


def place_pieces(here, pieces, shelf, whole):
    span = pieces[0].shape[1]
    for step, piece in enumerate(pieces):
        shelf[here ^ step] = piece[...]
    for at in range(len(pieces)):
        whole[:, at * span : (at + 1) * span] = shelf[at]


def hand_out(here, whole, shelf, pieces):
    span = pieces[0].shape[1]
    for at in range(len(pieces)):
        shelf[at] = whole[:, at * span : (at + 1) * span]
    for step, piece in enumerate(pieces):
        piece[...] = shelf[here ^ step]


def turned(rows):
    return rows.astype(f32).T.astype(bf16)


def forward_kernel(groups, lengths, here, *refs):
    pieces, refs = refs[:groups], refs[groups:]
    packed, mixed, totals = refs[:3]
    outs, refs = refs[3 : 3 + groups], refs[3 + groups :]
    shelf, out_shelf, key_rows = refs
    place_pieces(here[0], pieces, shelf, packed)
    key_rows[...] = turned(packed[HEAD : 2 * HEAD, :])
    for query_index in range(PASSES):
        query_span = slice(query_index * PASS_SLOTS, (query_index + 1) * PASS_SLOTS)
        queries = packed[:HEAD, query_span] * jnp.asarray(0.125, bf16)
        top = jnp.full((1, PASS_SLOTS), masked_value, f32)
        total = jnp.zeros((1, PASS_SLOTS), f32)
        acc = jnp.zeros((HEAD, PASS_SLOTS), f32)
        for key_index in range(query_index + 1):
            key_span = slice(key_index * PASS_SLOTS, (key_index + 1) * PASS_SLOTS)
            scores = contract(key_rows[key_span, :], queries, ((1,), (0,)))
            scores = jnp.where(tile_visible(lengths[0, key_index]), scores, masked_value)
            newest = jnp.maximum(top, jnp.max(scores, axis=0, keepdims=True))
            shares = jnp.exp(scores - newest)
            fade = jnp.exp(top - newest)
            total = total * fade + jnp.sum(shares, axis=0, keepdims=True)
            values = packed[2 * HEAD :, key_span]
            acc = acc * fade + contract(values, shares.astype(bf16), ((1,), (0,)))
            top = newest
        mixed[:, query_span] = (acc / total).astype(bf16)
        totals[query_index : query_index + 1, :] = top + jnp.log(total)
    hand_out(here[0], mixed, out_shelf, outs)


def backward_kernel(groups, lengths, here, packed, mixed, totals, *refs):
    pieces, refs = refs[:groups], refs[groups:]
    outs, refs = refs[:groups], refs[groups:]
    shelf, out_shelf, grad, rows, grad_rows, grad_query, result = refs
    place_pieces(here[0], pieces, shelf, grad)
    rows[...] = turned(packed[...])
    grad_rows[...] = turned(grad[...])
    grad_query[...] = jnp.zeros_like(grad_query)
    eighth = jnp.asarray(0.125, bf16)

    def key_pass(key_index, _):
        key_at = pl.multiple_of(key_index * PASS_SLOTS, PASS_SLOTS)
        key_span = pl.ds(key_at, PASS_SLOTS)
        keys = rows[key_span, HEAD : 2 * HEAD] * eighth
        keys_turned = packed[HEAD : 2 * HEAD, key_span] * eighth
        values = rows[key_span, 2 * HEAD :]
        shown = tile_visible(lengths[0, key_index])

        def query_pass(query_index, carried):
            grad_key, grad_value = carried
            query_at = pl.multiple_of(query_index * PASS_SLOTS, PASS_SLOTS)
            query_span = pl.ds(query_at, PASS_SLOTS)
            grads = grad[:, query_span]
            product = grads.astype(f32) * mixed[:, query_span].astype(f32)
            delta = jnp.sum(product, axis=0, keepdims=True)
            scores = contract(keys, packed[:HEAD, query_span], ((1,), (0,)))
            shares = jnp.exp(scores - totals[pl.ds(query_index, 1), :])
            shares = jnp.where(shown, shares, 0.0)
            grad_shares = contract(values, grads, ((1,), (0,)))
            grad_scores = (shares * (grad_shares - delta)).astype(bf16)
            grad_query[:, query_span] += contract(keys_turned, grad_scores, ((1,), (0,)))
            grad_value += contract(shares.astype(bf16), grad_rows[query_span, :], ((1,), (0,)))
            queries = rows[query_span, :HEAD] * eighth
            grad_key += contract(grad_scores, queries, ((1,), (0,)))
            return grad_key, grad_value

        empty = jnp.zeros((PASS_SLOTS, HEAD), f32)
        grad_key, grad_value = lax.fori_loop(key_index, PASSES, query_pass, (empty, empty))
        result[HEAD : 2 * HEAD, key_span] = grad_key.T.astype(bf16)
        result[2 * HEAD :, key_span] = grad_value.T.astype(bf16)
        return 0

    lax.fori_loop(0, PASSES, key_pass, 0)
    result[:HEAD, :] = grad_query[...].astype(bf16)
    hand_out(here[0], result, out_shelf, outs)


in_vmem = functools.partial(pl.BlockSpec, memory_space=pltpu.VMEM)
in_smem = functools.partial(pl.BlockSpec, memory_space=pltpu.SMEM)


def attend(lengths, here, pieces):
    groups = len(pieces)
    triple, span = pieces[0].shape
    slots = span * groups
    return pl.pallas_call(
        functools.partial(forward_kernel, groups),
        out_shape=[
            jax.ShapeDtypeStruct((triple, slots), bf16),
            jax.ShapeDtypeStruct((HEAD, slots), bf16),
            jax.ShapeDtypeStruct((PASSES, PASS_SLOTS), f32),
        ]
        + [jax.ShapeDtypeStruct((HEAD, span), bf16)] * groups,
        in_specs=[in_smem(), in_smem()] + [in_vmem()] * groups,
        out_specs=[in_vmem()] * (3 + groups),
        scratch_shapes=[
            pltpu.VMEM((groups, triple, span), bf16),
            pltpu.VMEM((groups, HEAD, span), bf16),
            pltpu.VMEM((slots, HEAD), bf16),
        ],
        compiler_params=pltpu.CompilerParams(vmem_limit_bytes=32 << 20),
        cost_estimate=pl.CostEstimate(flops=10**10, transcendentals=0, bytes_accessed=10**6),
        name="attend",
    )(lengths, here, *pieces)


def attend_back(lengths, here, packed, mixed, totals, pieces):
    groups = len(pieces)
    triple, slots = packed.shape
    span = slots // groups
    return pl.pallas_call(
        functools.partial(backward_kernel, groups),
        out_shape=[jax.ShapeDtypeStruct((triple, span), bf16)] * groups,
        in_specs=[in_smem(), in_smem()] + [in_vmem()] * (3 + groups),
        out_specs=[in_vmem()] * groups,
        scratch_shapes=[
            pltpu.VMEM((groups, HEAD, span), bf16),
            pltpu.VMEM((groups, triple, span), bf16),
            pltpu.VMEM((HEAD, slots), bf16),
            pltpu.VMEM((slots, triple), bf16),
            pltpu.VMEM((slots, HEAD), bf16),
            pltpu.VMEM((HEAD, slots), f32),
            pltpu.VMEM((triple, slots), bf16),
        ],
        compiler_params=pltpu.CompilerParams(vmem_limit_bytes=32 << 20),
        cost_estimate=pl.CostEstimate(
            flops=15 * 10**9, transcendentals=0, bytes_accessed=10**6
        ),
        name="attend_back",
    )(lengths, here, packed, mixed, totals, *pieces)


def row_major(values):
    return with_layout_constraint(values, Layout(tuple(range(values.ndim))))


def after(values, *others):
    return lax.optimization_barrier((values, others))[0]


def swap_with(values, axis, step):
    size = lax.axis_size(axis)
    return lax.ppermute(values, axis, [(i, i ^ step) for i in range(size)])


def axis_bits(axis):
    size = lax.axis_size(axis)
    assert size & (size - 1) == 0
    return [(axis, 1 << n) for n in reversed(range(size.bit_length() - 1))]


def bit_order(flip):
    places = axis_bits("seq") + axis_bits("blk")
    near = axis_bits("seq")
    far = near[:-1][::-1] if flip else near[:-1]
    return places, axis_bits("blk") + far + near[-1:]


def own_bit(bit):
    return (lax.axis_index(bit[0]) & bit[1]) != 0


class Gather:
    def __init__(self, piece, flip):
        self.places, self.order = bit_order(flip)
        self.shape = piece.shape
        self.piece = piece
        self.done = []

    def grow(self, count=None):
        count = len(self.order) if count is None else count
        for bit in self.order[:count]:
            other = swap_with(self.piece, *bit)
            self.done = sorted(self.done + [bit], key=self.places.index)
            mine = own_bit(bit)
            low = jnp.where(mine, other, self.piece)
            high = jnp.where(mine, self.piece, other)
            self.piece = jnp.stack([low, high], axis=self.done.index(bit))
        self.order = self.order[count:]
        return self.piece

    def whole(self):
        return self.grow().reshape((-1,) + self.shape[1:])


class Scatter:
    def __init__(self, whole, flip):
        self.left, order = bit_order(flip)
        self.order = order[::-1]
        self.sent = None
        rows = whole.shape[0] >> len(order)
        self.piece = whole.reshape((2,) * len(order) + (rows,) + whole.shape[1:])

    def send(self):
        bit, self.order = self.order[0], self.order[1:]
        at = self.left.index(bit)
        self.left = [place for place in self.left if place != bit]
        low = lax.index_in_dim(self.piece, 0, at, keepdims=False)
        high = lax.index_in_dim(self.piece, 1, at, keepdims=False)
        mine = own_bit(bit)
        self.bit = bit
        self.sent = jnp.where(mine, low, high)
        self.kept = jnp.where(mine, high, low)
        return (self.sent, self.kept)

    def receive(self, *others):
        if self.sent is None:
            return
        other = after(swap_with(self.sent, *self.bit), others)
        self.sent = None
        self.piece = (self.kept.astype(f32) + other.astype(f32)).astype(bf16)

    def finish(self):
        self.receive()
        while self.order:
            self.send()
            self.receive()
        return self.piece


def swap_pieces(pieces):
    return [swap_with(piece, "blk", step) if step else piece for step, piece in enumerate(pieces)]


def in_order(pieces):
    here = lax.axis_index("blk")
    result = jnp.zeros((len(pieces),) + pieces[0].shape, pieces[0].dtype)
    for step, piece in enumerate(pieces):
        result = lax.dynamic_update_index_in_dim(result, piece, here ^ step, 0)
    return result


def at_group(values, group):
    return lax.dynamic_index_in_dim(values, group, 0, keepdims=False)


def by_head(rows, groups):
    count = rows.shape[0]
    return rows.reshape(count, 3, groups, -1, HEAD).transpose(0, 3, 2, 1, 4).reshape(count, -1)


def by_kind(rows, groups):
    count = rows.shape[0]
    return rows.reshape(count, -1, groups, 3, HEAD).transpose(0, 3, 2, 1, 4).reshape(count, -1)


def norm_parts(values):
    centre = values - jnp.mean(values, axis=-1, keepdims=True)
    spread = jnp.mean(centre * centre, axis=-1, keepdims=True)
    scale = lax.rsqrt(spread + 1e-05)
    return centre * scale, scale


def norm_back(values, gain, grad):
    hat, scale = norm_parts(values)
    edge = grad * gain
    part = scale * (
        edge
        - jnp.mean(edge, axis=-1, keepdims=True)
        - hat * jnp.mean(edge * hat, axis=-1, keepdims=True)
    )
    return part, jnp.sum(grad * hat, axis=0), jnp.sum(grad, axis=0)


def on_device(states, cotangent, lengths, w_qkv, w_out, w_up, w_down, vectors, up_bias):
    _, row_count, width = states.shape
    groups = lax.axis_size("blk")
    own = w_qkv.shape[0]
    wide = w_up.shape[1]
    ratio = wide // width
    vector_count = vectors.shape[0]
    heads = width // HEAD // groups
    span = 3 * HEAD
    small = vector_count + ratio

    here = lax.axis_index("blk").astype(jnp.int32)
    parts = by_head(w_qkv, groups)
    middle_column = parts.shape[1] // 2
    extra = [vectors.T, up_bias.reshape(own, ratio), jnp.zeros((own, -small % 128), bf16)]
    streams = [
        Gather(jnp.concatenate([parts[:, :middle_column]] + extra, axis=1), False),
        Gather(parts[:, middle_column:], True),
    ]
    blk_steps = len(axis_bits("blk"))
    begun = [stream.grow(blk_steps) for stream in streams]
    w_out, w_up, w_down = after((w_out, w_up, w_down), begun)
    later = [Gather(w_up, False), Gather(w_down, True), Gather(w_out, False)]
    for one in later:
        one.grow(1)
    first = [stream.whole() for stream in streams]
    for one in later:
        one.piece = after(one.piece, first)
        one.grow(blk_steps - 1)
    full_qkv = jnp.concatenate([first[0][:, :middle_column], first[1]], axis=1)
    head_qkv = [full_qkv[:, h * groups * span : (h + 1) * groups * span] for h in range(heads)]
    corner = first[0][:, middle_column : middle_column + small]
    table = corner[:, :vector_count].astype(f32).T
    bias_up = corner[:, vector_count:].astype(f32).reshape(wide)

    slots = lax.axis_index("blk") * row_count + jnp.arange(row_count, dtype=jnp.int32)
    pass_of = (slots // PASS_SLOTS)[:, None] == jnp.arange(PASSES, dtype=jnp.int32)[None, :]
    bounds = jnp.sum(jnp.where(pass_of, lengths[0][None, :], 0), axis=1)
    live = (slots % PASS_SLOTS < bounds).astype(f32)[:, None]

    added = jnp.zeros((row_count, width), f32)
    for index in range(PASSES):
        added = jnp.where(pass_of[:, index : index + 1], table[index], added)
    start = states[0].astype(f32) + added
    normed_a = layer_norm(start, table[5], table[6]).astype(bf16)
    column = jnp.arange(3 * width, dtype=jnp.int32)
    kind = column // HEAD % 3
    source = (column // span % groups) * heads + column // (span * groups)
    source = source * HEAD + column % HEAD
    match = source[:, None] == jnp.arange(width, dtype=jnp.int32)[None, :]
    choice = jnp.where((kind == 0)[:, None], table[7], jnp.where((kind == 2)[:, None], table[8], 0.0))
    bias_three = jnp.sum(jnp.where(match, choice, 0.0), axis=1, keepdims=True)
    bias_three = bias_three.reshape(heads, -1, 1)
    sending = []
    for h in range(heads):
        rows = contract(head_qkv[h], normed_a, ((0,), (1,))) + bias_three[h]
        rows = rows.astype(bf16).reshape(groups, span, row_count)
        sending.append([row_major(at_group(rows, here ^ step)) for step in range(groups)])
    for one in later:
        one.piece = after(one.piece, sending)
    kept = []
    arrived = []
    returned = []
    for h in range(heads):
        pieces = swap_pieces(after(sending[h], arrived))
        arrived = pieces
        packed, mixed, totals, *pieces = attend(lengths, here[None], pieces)
        kept.append((packed, mixed, totals))
        returned.append(swap_pieces(pieces))
    full_up, full_down, full_out = [one.whole() for one in later]
    returned[:-1] = after(returned[:-1], pieces)
    returned = [in_order(pieces) for pieces in returned]
    heads_out = jnp.stack(returned, axis=1).reshape(width, row_count)
    middle = start + live * (contract(heads_out, full_out, ((0,), (0,))) + table[9])
    normed_b = layer_norm(middle, table[10], table[11]).astype(bf16)
    up_sum = contract(normed_b, full_up, ((1,), (0,))) + bias_up
    activated, gelu_pull = jax.vjp(gelu_tanh, up_sum)
    hidden = activated.astype(bf16)
    incoming = cotangent[0].astype(f32)
    grad_branch = (live * incoming).astype(bf16)
    grad_hidden = contract(grad_branch, full_down, ((1,), (1,)))
    grad_upsum = gelu_pull(grad_hidden)[0].astype(bf16)
    grad_normb = contract(grad_upsum, full_up, ((1,), (1,)))
    middle_part, gain_grad_b, shift_grad_b = norm_back(middle, table[10], grad_normb)
    grad_middle = incoming + middle_part
    grad_attn = (live * grad_middle).astype(bf16)
    grad_heads = contract(full_out, grad_attn, ((1,), (1,))).astype(bf16)
    grad_heads = grad_heads.reshape(groups, heads, HEAD, row_count)
    sending = [
        [row_major(at_group(grad_heads[:, h], here ^ step)) for step in range(groups)]
        for h in range(heads)
    ]
    arrived = []
    late = []
    parts = []
    for h in range(heads):
        pieces = swap_pieces(after(sending[h], arrived))
        arrived = pieces
        if late:
            if h > 1:
                for one in late:
                    one.receive(parts[-1])
            pieces = after(pieces, [one.send() for one in late])
        back = attend_back(lengths, here[None], *kept[h], pieces)
        if not late:
            hidden_late, grad_branch_late, grad_upsum_late, grad_attn_late = after(
                (hidden, grad_branch, grad_upsum, grad_attn), back
            )
            grad_down = contract(hidden_late, grad_branch_late, ((0,), (0,))).astype(bf16)
            grad_up = contract(normed_b, grad_upsum_late, ((0,), (0,))).astype(bf16)
            grad_out = contract(heads_out, grad_attn_late, ((1,), (0,))).astype(bf16)
            grad_up = jnp.concatenate([grad_up, grad_out], axis=1)
            late = [Scatter(grad_down, True), Scatter(grad_up, False)]
        parts.append(back)
    grad_projected = [swap_pieces(back) for back in parts]
    grad_projected[:-1] = after(grad_projected[:-1], parts[-1])
    for one in late:
        one.receive(parts[-1])
    sent = [one.send() for one in late]
    outcome = middle + live * (contract(hidden, full_down, ((1,), (0,))) + table[12])

    whole = [in_order(pieces).reshape(groups * span, row_count) for pieces in grad_projected[:-1]]
    early = [contract(normed_a, part, ((0,), (1,))).astype(bf16) for part in whole]
    early = Scatter(after(jnp.concatenate(early, axis=1), sent), True)
    pieces = after(grad_projected[-1], early.send())
    whole.append(in_order(pieces).reshape(groups * span, row_count))
    final = contract(normed_a, whole[-1], ((0,), (1,))).astype(bf16)
    grad_norma = sum(contract(part, weights, ((0,), (1,))) for part, weights in zip(whole, head_qkv))
    started = early.sent
    early.receive(whole[-1])
    sent = [early.send()]
    for one in late:
        one.receive(started)
        sent.append(one.send())
    grad_norma = after(grad_norma, sent)
    sums = [jnp.sum(part.astype(f32), axis=1) for part in whole]
    column_sums = by_kind(jnp.concatenate(sums)[None], groups)[0]
    start_part, gain_grad_a, shift_grad_a = norm_back(start, table[5], grad_norma)
    grad_start = grad_middle + start_part
    grad_embed = [
        jnp.sum(jnp.where(pass_of[:, index : index + 1], grad_start, 0.0), axis=0)
        for index in range(PASSES)
    ]
    vector_grads = jnp.stack(
        grad_embed
        + [
            gain_grad_a,
            shift_grad_a,
            column_sums[:width],
            column_sums[2 * width :],
            jnp.sum(grad_attn.astype(f32), axis=0),
            gain_grad_b,
            shift_grad_b,
            jnp.sum(grad_branch.astype(f32), axis=0),
        ]
    )
    bias_grads = jnp.sum(grad_upsum.astype(f32), axis=0)
    extra = [vector_grads.T.astype(bf16), bias_grads.reshape(width, ratio).astype(bf16)]
    last = Scatter(jnp.concatenate([final] + extra + [jnp.zeros((width, -small % 128), bf16)], axis=1), False)
    wave = 0
    tied = last.send()
    early.receive(tied)
    while last.order:
        sent = [early.send()] if early.order else []
        if wave % 2 == 1 and late[0].order:
            for one in late:
                one.receive(tied)
                sent.append(one.send())
        last.receive(sent)
        tied = last.send()
        early.receive(tied)
        wave += 1
    last.receive()
    for one in late:
        one.receive(tied)
        one.finish()
    grad_down = late[0].piece
    grad_up = late[1].piece[:, :wide]
    grad_out = late[1].piece[:, wide:]
    grad_qkv = [early.finish(), last.piece[:, : groups * span]]
    extra = last.piece[:, groups * span :].astype(f32)
    return (
        outcome.astype(bf16)[None],
        grad_start.astype(bf16)[None],
        by_kind(jnp.concatenate(grad_qkv, axis=1).astype(f32), groups),
        grad_out.astype(f32),
        grad_up.astype(f32),
        grad_down.astype(f32),
        extra[:, :vector_count].T,
        extra[:, vector_count:small].reshape(own * ratio),
    )


def solution(mesh):
    split = P(both, None)
    return jax.shard_map(
        on_device,
        mesh=mesh,
        in_specs=(
            P("seq", "blk", None),
            P("seq", "blk", None),
            P("seq", None),
            split,
            split,
            split,
            split,
            P(None, both),
            P(both),
        ),
        out_specs=(
            P("seq", "blk", None),
            P("seq", "blk", None),
            split,
            split,
            split,
            split,
            P(None, both),
            P(both),
        ),
        check_vma=False,
    )
```

```python
import functools

import jax
import jax.numpy as jnp
from jax import lax
from jax.experimental import pallas as pl
from jax.experimental.layout import Layout, with_layout_constraint
from jax.experimental.pallas import tpu as pltpu
from jax.sharding import PartitionSpec as P


HEAD = 64
PASSES = 5
PASS_SLOTS = 512


masked_value = -1e30
both = ("seq", "blk")
f32 = jnp.float32
bf16 = jnp.bfloat16


def layer_norm(values, gain, offset):
    centre = values - jnp.mean(values, axis=-1, keepdims=True)
    spread = jnp.mean(centre * centre, axis=-1, keepdims=True)
    return centre * lax.rsqrt(spread + 1e-05) * gain + offset


def gelu_tanh(values):
    return jax.nn.gelu(values, approximate=True)


def contract(left, right, dims):
    return lax.dot_general(left, right, (dims, ((), ())), preferred_element_type=f32)


def tile_visible(length):
    key_place = lax.broadcasted_iota(jnp.int32, (PASS_SLOTS, PASS_SLOTS), 0)
    query_place = lax.broadcasted_iota(jnp.int32, (PASS_SLOTS, PASS_SLOTS), 1)
    return (key_place <= query_place) & (key_place < length)


def place_pieces(here, pieces, shelf, whole):
    span = pieces[0].shape[1]
    for step, piece in enumerate(pieces):
        shelf[here ^ step] = piece[...]
    for at in range(len(pieces)):
        whole[:, at * span : (at + 1) * span] = shelf[at]


def hand_out(here, whole, shelf, pieces):
    span = pieces[0].shape[1]
    for at in range(len(pieces)):
        shelf[at] = whole[:, at * span : (at + 1) * span]
    for step, piece in enumerate(pieces):
        piece[...] = shelf[here ^ step]


def turned(rows):
    return rows.astype(f32).T.astype(bf16)


def forward_kernel(groups, lengths, here, *refs):
    pieces, refs = refs[:groups], refs[groups:]
    packed, mixed, totals = refs[:3]
    outs, refs = refs[3 : 3 + groups], refs[3 + groups :]
    shelf, out_shelf, key_rows = refs
    place_pieces(here[0], pieces, shelf, packed)
    key_rows[...] = turned(packed[HEAD : 2 * HEAD, :])
    for query_index in range(PASSES):
        query_span = slice(query_index * PASS_SLOTS, (query_index + 1) * PASS_SLOTS)
        queries = packed[:HEAD, query_span] * jnp.asarray(0.125, bf16)
        top = jnp.full((1, PASS_SLOTS), masked_value, f32)
        total = jnp.zeros((1, PASS_SLOTS), f32)
        acc = jnp.zeros((HEAD, PASS_SLOTS), f32)
        for key_index in range(query_index + 1):
            key_span = slice(key_index * PASS_SLOTS, (key_index + 1) * PASS_SLOTS)
            scores = contract(key_rows[key_span, :], queries, ((1,), (0,)))
            scores = jnp.where(tile_visible(lengths[0, key_index]), scores, masked_value)
            newest = jnp.maximum(top, jnp.max(scores, axis=0, keepdims=True))
            shares = jnp.exp(scores - newest)
            fade = jnp.exp(top - newest)
            total = total * fade + jnp.sum(shares, axis=0, keepdims=True)
            values = packed[2 * HEAD :, key_span]
            acc = acc * fade + contract(values, shares.astype(bf16), ((1,), (0,)))
            top = newest
        mixed[:, query_span] = (acc / total).astype(bf16)
        totals[query_index : query_index + 1, :] = top + jnp.log(total)
    hand_out(here[0], mixed, out_shelf, outs)


def backward_kernel(groups, lengths, here, packed, mixed, totals, *refs):
    pieces, refs = refs[:groups], refs[groups:]
    outs, refs = refs[:groups], refs[groups:]
    shelf, out_shelf, grad, rows, grad_rows, grad_query, result = refs
    place_pieces(here[0], pieces, shelf, grad)
    rows[...] = turned(packed[...])
    grad_rows[...] = turned(grad[...])
    grad_query[...] = jnp.zeros_like(grad_query)
    eighth = jnp.asarray(0.125, bf16)

    def key_pass(key_index, _):
        key_at = pl.multiple_of(key_index * PASS_SLOTS, PASS_SLOTS)
        key_span = pl.ds(key_at, PASS_SLOTS)
        keys = rows[key_span, HEAD : 2 * HEAD] * eighth
        keys_turned = packed[HEAD : 2 * HEAD, key_span] * eighth
        values = rows[key_span, 2 * HEAD :]
        shown = tile_visible(lengths[0, key_index])

        def query_pass(query_index, carried):
            grad_key, grad_value = carried
            query_at = pl.multiple_of(query_index * PASS_SLOTS, PASS_SLOTS)
            query_span = pl.ds(query_at, PASS_SLOTS)
            grads = grad[:, query_span]
            product = grads.astype(f32) * mixed[:, query_span].astype(f32)
            delta = jnp.sum(product, axis=0, keepdims=True)
            scores = contract(keys, packed[:HEAD, query_span], ((1,), (0,)))
            shares = jnp.exp(scores - totals[pl.ds(query_index, 1), :])
            shares = jnp.where(shown, shares, 0.0)
            grad_shares = contract(values, grads, ((1,), (0,)))
            grad_scores = (shares * (grad_shares - delta)).astype(bf16)
            grad_query[:, query_span] += contract(keys_turned, grad_scores, ((1,), (0,)))
            grad_value += contract(shares.astype(bf16), grad_rows[query_span, :], ((1,), (0,)))
            queries = rows[query_span, :HEAD] * eighth
            grad_key += contract(grad_scores, queries, ((1,), (0,)))
            return grad_key, grad_value

        empty = jnp.zeros((PASS_SLOTS, HEAD), f32)
        grad_key, grad_value = lax.fori_loop(key_index, PASSES, query_pass, (empty, empty))
        result[HEAD : 2 * HEAD, key_span] = grad_key.T.astype(bf16)
        result[2 * HEAD :, key_span] = grad_value.T.astype(bf16)
        return 0

    lax.fori_loop(0, PASSES, key_pass, 0)
    result[:HEAD, :] = grad_query[...].astype(bf16)
    hand_out(here[0], result, out_shelf, outs)


in_vmem = functools.partial(pl.BlockSpec, memory_space=pltpu.VMEM)
in_smem = functools.partial(pl.BlockSpec, memory_space=pltpu.SMEM)


def attend(lengths, here, pieces):
    groups = len(pieces)
    triple, span = pieces[0].shape
    slots = span * groups
    return pl.pallas_call(
        functools.partial(forward_kernel, groups),
        out_shape=[
            jax.ShapeDtypeStruct((triple, slots), bf16),
            jax.ShapeDtypeStruct((HEAD, slots), bf16),
            jax.ShapeDtypeStruct((PASSES, PASS_SLOTS), f32),
        ]
        + [jax.ShapeDtypeStruct((HEAD, span), bf16)] * groups,
        in_specs=[in_smem(), in_smem()] + [in_vmem()] * groups,
        out_specs=[in_vmem()] * (3 + groups),
        scratch_shapes=[
            pltpu.VMEM((groups, triple, span), bf16),
            pltpu.VMEM((groups, HEAD, span), bf16),
            pltpu.VMEM((slots, HEAD), bf16),
        ],
        compiler_params=pltpu.CompilerParams(vmem_limit_bytes=32 << 20),
        cost_estimate=pl.CostEstimate(flops=10**10, transcendentals=0, bytes_accessed=10**6),
        name="attend",
    )(lengths, here, *pieces)


def attend_back(lengths, here, packed, mixed, totals, pieces):
    groups = len(pieces)
    triple, slots = packed.shape
    span = slots // groups
    return pl.pallas_call(
        functools.partial(backward_kernel, groups),
        out_shape=[jax.ShapeDtypeStruct((triple, span), bf16)] * groups,
        in_specs=[in_smem(), in_smem()] + [in_vmem()] * (3 + groups),
        out_specs=[in_vmem()] * groups,
        scratch_shapes=[
            pltpu.VMEM((groups, HEAD, span), bf16),
            pltpu.VMEM((groups, triple, span), bf16),
            pltpu.VMEM((HEAD, slots), bf16),
            pltpu.VMEM((slots, triple), bf16),
            pltpu.VMEM((slots, HEAD), bf16),
            pltpu.VMEM((HEAD, slots), f32),
            pltpu.VMEM((triple, slots), bf16),
        ],
        compiler_params=pltpu.CompilerParams(vmem_limit_bytes=32 << 20),
        cost_estimate=pl.CostEstimate(
            flops=15 * 10**9, transcendentals=0, bytes_accessed=10**6
        ),
        name="attend_back",
    )(lengths, here, packed, mixed, totals, *pieces)


def row_major(values):
    return with_layout_constraint(values, Layout(tuple(range(values.ndim))))


def after(values, *others):
    return lax.optimization_barrier((values, others))[0]


def swap_with(values, axis, step):
    size = lax.axis_size(axis)
    return lax.ppermute(values, axis, [(i, i ^ step) for i in range(size)])


def axis_bits(axis):
    size = lax.axis_size(axis)
    assert size & (size - 1) == 0
    return [(axis, 1 << n) for n in reversed(range(size.bit_length() - 1))]


def bit_order(flip):
    places = axis_bits("seq") + axis_bits("blk")
    near = axis_bits("seq")
    far = near[:-1][::-1] if flip else near[:-1]
    return places, axis_bits("blk") + far + near[-1:]


def own_bit(bit):
    return (lax.axis_index(bit[0]) & bit[1]) != 0


class Gather:
    def __init__(self, piece, flip):
        self.places, self.order = bit_order(flip)
        self.shape = piece.shape
        self.piece = piece
        self.done = []

    def grow(self, count=None):
        count = len(self.order) if count is None else count
        for bit in self.order[:count]:
            other = swap_with(self.piece, *bit)
            self.done = sorted(self.done + [bit], key=self.places.index)
            mine = own_bit(bit)
            low = jnp.where(mine, other, self.piece)
            high = jnp.where(mine, self.piece, other)
            self.piece = jnp.stack([low, high], axis=self.done.index(bit))
        self.order = self.order[count:]
        return self.piece

    def whole(self):
        return self.grow().reshape((-1,) + self.shape[1:])


class Scatter:
    def __init__(self, whole, flip):
        self.left, order = bit_order(flip)
        self.order = order[::-1]
        self.sent = None
        rows = whole.shape[0] >> len(order)
        self.piece = whole.reshape((2,) * len(order) + (rows,) + whole.shape[1:])

    def send(self):
        bit, self.order = self.order[0], self.order[1:]
        at = self.left.index(bit)
        self.left = [place for place in self.left if place != bit]
        low = lax.index_in_dim(self.piece, 0, at, keepdims=False)
        high = lax.index_in_dim(self.piece, 1, at, keepdims=False)
        mine = own_bit(bit)
        self.bit = bit
        self.sent = jnp.where(mine, low, high)
        self.kept = jnp.where(mine, high, low)
        return (self.sent, self.kept)

    def receive(self, *others):
        if self.sent is None:
            return
        other = after(swap_with(self.sent, *self.bit), others)
        self.sent = None
        self.piece = (self.kept.astype(f32) + other.astype(f32)).astype(bf16)

    def finish(self):
        self.receive()
        while self.order:
            self.send()
            self.receive()
        return self.piece


def swap_pieces(pieces):
    return [swap_with(piece, "blk", step) if step else piece for step, piece in enumerate(pieces)]


def in_order(pieces):
    here = lax.axis_index("blk")
    result = jnp.zeros((len(pieces),) + pieces[0].shape, pieces[0].dtype)
    for step, piece in enumerate(pieces):
        result = lax.dynamic_update_index_in_dim(result, piece, here ^ step, 0)
    return result


def at_group(values, group):
    return lax.dynamic_index_in_dim(values, group, 0, keepdims=False)


def by_head(rows, groups):
    count = rows.shape[0]
    return rows.reshape(count, 3, groups, -1, HEAD).transpose(0, 3, 2, 1, 4).reshape(count, -1)


def by_kind(rows, groups):
    count = rows.shape[0]
    return rows.reshape(count, -1, groups, 3, HEAD).transpose(0, 3, 2, 1, 4).reshape(count, -1)


def norm_parts(values):
    centre = values - jnp.mean(values, axis=-1, keepdims=True)
    spread = jnp.mean(centre * centre, axis=-1, keepdims=True)
    scale = lax.rsqrt(spread + 1e-05)
    return centre * scale, scale


def norm_back(values, gain, grad):
    hat, scale = norm_parts(values)
    edge = grad * gain
    part = scale * (
        edge
        - jnp.mean(edge, axis=-1, keepdims=True)
        - hat * jnp.mean(edge * hat, axis=-1, keepdims=True)
    )
    return part, jnp.sum(grad * hat, axis=0), jnp.sum(grad, axis=0)


def on_device(states, cotangent, lengths, w_qkv, w_out, w_up, w_down, vectors, up_bias):
    _, row_count, width = states.shape
    groups = lax.axis_size("blk")
    own = w_qkv.shape[0]
    wide = w_up.shape[1]
    ratio = wide // width
    vector_count = vectors.shape[0]
    heads = width // HEAD // groups
    span = 3 * HEAD
    small = vector_count + ratio

    here = lax.axis_index("blk").astype(jnp.int32)
    parts = by_head(w_qkv, groups)
    middle_column = parts.shape[1] // 2
    extra = [vectors.T, up_bias.reshape(own, ratio), jnp.zeros((own, -small % 128), bf16)]
    streams = [
        Gather(jnp.concatenate([parts[:, :middle_column]] + extra, axis=1), False),
        Gather(parts[:, middle_column:], True),
    ]
    blk_steps = len(axis_bits("blk"))
    begun = [stream.grow(blk_steps) for stream in streams]
    w_out, w_up, w_down = after((w_out, w_up, w_down), begun)
    later = [Gather(w_up, False), Gather(w_down, True), Gather(w_out, False)]
    for one in later:
        one.grow(blk_steps)
    first = [stream.whole() for stream in streams]
    for one in later:
        one.piece = after(one.piece, first)
        one.grow(1)
    full_qkv = jnp.concatenate([first[0][:, :middle_column], first[1]], axis=1)
    head_qkv = [full_qkv[:, h * groups * span : (h + 1) * groups * span] for h in range(heads)]
    corner = first[0][:, middle_column : middle_column + small]
    table = corner[:, :vector_count].astype(f32).T
    bias_up = corner[:, vector_count:].astype(f32).reshape(wide)

    slots = lax.axis_index("blk") * row_count + jnp.arange(row_count, dtype=jnp.int32)
    pass_of = (slots // PASS_SLOTS)[:, None] == jnp.arange(PASSES, dtype=jnp.int32)[None, :]
    bounds = jnp.sum(jnp.where(pass_of, lengths[0][None, :], 0), axis=1)
    live = (slots % PASS_SLOTS < bounds).astype(f32)[:, None]

    added = jnp.zeros((row_count, width), f32)
    for index in range(PASSES):
        added = jnp.where(pass_of[:, index : index + 1], table[index], added)
    start = states[0].astype(f32) + added
    normed_a = layer_norm(start, table[5], table[6]).astype(bf16)
    column = jnp.arange(3 * width, dtype=jnp.int32)
    kind = column // HEAD % 3
    source = (column // span % groups) * heads + column // (span * groups)
    source = source * HEAD + column % HEAD
    match = source[:, None] == jnp.arange(width, dtype=jnp.int32)[None, :]
    choice = jnp.where((kind == 0)[:, None], table[7], jnp.where((kind == 2)[:, None], table[8], 0.0))
    bias_three = jnp.sum(jnp.where(match, choice, 0.0), axis=1, keepdims=True)
    bias_three = bias_three.reshape(heads, -1, 1)
    sending = []
    for h in range(heads):
        rows = contract(head_qkv[h], normed_a, ((0,), (1,))) + bias_three[h]
        rows = rows.astype(bf16).reshape(groups, span, row_count)
        sending.append([row_major(at_group(rows, here ^ step)) for step in range(groups)])
    for one in later:
        one.piece = after(one.piece, sending[0])
    kept = []
    arrived = []
    returned = []
    for h in range(heads):
        pieces = swap_pieces(after(sending[h], arrived))
        arrived = pieces
        if h == 1:
            pieces = after(pieces, [one.piece for one in later])
        packed, mixed, totals, *pieces = attend(lengths, here[None], pieces)
        kept.append((packed, mixed, totals))
        returned.append(swap_pieces(pieces))
    full_up, full_down, full_out = [one.whole() for one in later]
    returned[:-1] = after(returned[:-1], pieces)
    returned = [in_order(pieces) for pieces in returned]
    heads_out = jnp.stack(returned, axis=1).reshape(width, row_count)
    middle = start + live * (contract(heads_out, full_out, ((0,), (0,))) + table[9])
    normed_b = layer_norm(middle, table[10], table[11]).astype(bf16)
    up_sum = contract(normed_b, full_up, ((1,), (0,))) + bias_up
    activated, gelu_pull = jax.vjp(gelu_tanh, up_sum)
    hidden = activated.astype(bf16)
    outcome = middle + live * (contract(hidden, full_down, ((1,), (0,))) + table[12])
    incoming = cotangent[0].astype(f32)
    grad_branch = (live * incoming).astype(bf16)
    grad_hidden = contract(grad_branch, full_down, ((1,), (1,)))
    grad_upsum = gelu_pull(grad_hidden)[0].astype(bf16)
    grad_normb = contract(grad_upsum, full_up, ((1,), (1,)))
    middle_part, gain_grad_b, shift_grad_b = norm_back(middle, table[10], grad_normb)
    grad_middle = incoming + middle_part
    grad_attn = (live * grad_middle).astype(bf16)
    grad_heads = contract(full_out, grad_attn, ((1,), (1,))).astype(bf16)
    grad_heads = grad_heads.reshape(groups, heads, HEAD, row_count)
    sending = [
        [row_major(at_group(grad_heads[:, h], here ^ step)) for step in range(groups)]
        for h in range(heads)
    ]
    arrived = []
    late = []
    parts = []
    for h in range(heads):
        pieces = swap_pieces(after(sending[h], arrived))
        arrived = pieces
        if h == 0:
            pieces = after(pieces, outcome)
        if late:
            if h > 1:
                for one in late:
                    one.receive(parts[-1])
            pieces = after(pieces, [one.send() for one in late])
        back = attend_back(lengths, here[None], *kept[h], pieces)
        if not late:
            hidden_late, grad_branch_late, grad_upsum_late, grad_attn_late = after(
                (hidden, grad_branch, grad_upsum, grad_attn), back
            )
            grad_down = contract(hidden_late, grad_branch_late, ((0,), (0,))).astype(bf16)
            grad_up = contract(normed_b, grad_upsum_late, ((0,), (0,))).astype(bf16)
            grad_out = contract(heads_out, grad_attn_late, ((1,), (0,))).astype(bf16)
            grad_up = jnp.concatenate([grad_up, grad_out], axis=1)
            late = [Scatter(grad_down, True), Scatter(grad_up, False)]
        parts.append(back)
    grad_projected = []
    for back in parts:
        grad_projected.append(swap_pieces(back))
    grad_projected[:-1] = after(grad_projected[:-1], parts[-1])
    for one in late:
        one.receive(parts[-1])
    sent = [one.send() for one in late]

    whole = [in_order(pieces).reshape(groups * span, row_count) for pieces in grad_projected[:-1]]
    early = [row_major(contract(normed_a, part, ((0,), (1,))).astype(bf16)) for part in whole]
    early = Scatter(after(jnp.concatenate(early, axis=1), sent), True)
    pieces = after(grad_projected[-1], early.send())
    whole.append(in_order(pieces).reshape(groups * span, row_count))
    final = row_major(contract(normed_a, whole[-1], ((0,), (1,))).astype(bf16))
    grad_norma = sum(contract(part, weights, ((0,), (1,))) for part, weights in zip(whole, head_qkv))
    started = early.sent
    early.receive(whole[-1])
    sent = [early.send()]
    for one in late:
        one.receive(started)
        sent.append(one.send())
    grad_norma = after(grad_norma, sent)
    sums = [jnp.sum(part.astype(f32), axis=1) for part in whole]
    column_sums = by_kind(jnp.concatenate(sums)[None], groups)[0]
    start_part, gain_grad_a, shift_grad_a = norm_back(start, table[5], grad_norma)
    grad_start = grad_middle + start_part
    grad_embed = [
        jnp.sum(jnp.where(pass_of[:, index : index + 1], grad_start, 0.0), axis=0)
        for index in range(PASSES)
    ]
    vector_grads = jnp.stack(
        grad_embed
        + [
            gain_grad_a,
            shift_grad_a,
            column_sums[:width],
            column_sums[2 * width :],
            jnp.sum(grad_attn.astype(f32), axis=0),
            gain_grad_b,
            shift_grad_b,
            jnp.sum(grad_branch.astype(f32), axis=0),
        ]
    )
    bias_grads = jnp.sum(grad_upsum.astype(f32), axis=0)
    extra = [vector_grads.T.astype(bf16), bias_grads.reshape(width, ratio).astype(bf16)]
    last = Scatter(jnp.concatenate([final] + extra + [jnp.zeros((width, -small % 128), bf16)], axis=1), False)
    wave = 0
    tied = last.send()
    early.receive(tied)
    while last.order:
        sent = [early.send()] if early.order else []
        if wave % 2 == 0 and late[0].order:
            for one in late:
                one.receive(tied)
                sent.append(one.send())
        elif not late[0].order:
            for one in late:
                one.receive(tied)
                sent.append(one.piece)
        last.receive(sent)
        tied = last.send()
        early.receive(tied)
        wave += 1
    last.receive()
    for one in late:
        one.receive(tied)
        one.finish()
    grad_down = late[0].piece
    grad_up = late[1].piece[:, :wide]
    grad_out = late[1].piece[:, wide:]
    grad_qkv = [early.finish(), last.piece[:, : groups * span]]
    extra = last.piece[:, groups * span :].astype(f32)
    return (
        outcome.astype(bf16)[None],
        grad_start.astype(bf16)[None],
        by_kind(jnp.concatenate(grad_qkv, axis=1).astype(f32), groups),
        grad_out.astype(f32),
        grad_up.astype(f32),
        grad_down.astype(f32),
        extra[:, :vector_count].T,
        extra[:, vector_count:small].reshape(own * ratio),
    )


def solution(mesh):
    split = P(both, None)
    return jax.shard_map(
        on_device,
        mesh=mesh,
        in_specs=(
            P("seq", "blk", None),
            P("seq", "blk", None),
            P("seq", None),
            split,
            split,
            split,
            split,
            P(None, both),
            P(both),
        ),
        out_specs=(
            P("seq", "blk", None),
            P("seq", "blk", None),
            split,
            split,
            split,
            split,
            P(None, both),
            P(both),
        ),
        check_vma=False,
    )
```

```python
import functools

import jax
import jax.numpy as jnp
from jax import lax
from jax.experimental import pallas as pl
from jax.experimental.layout import Layout, with_layout_constraint
from jax.experimental.pallas import tpu as pltpu
from jax.sharding import PartitionSpec as P


HEAD = 64
PASSES = 5
PASS_SLOTS = 512
PART = 256


masked_value = -1e30
both = ("seq", "blk")
f32 = jnp.float32
bf16 = jnp.bfloat16


def layer_norm(values, gain, offset):
    centre = values - jnp.mean(values, axis=-1, keepdims=True)
    spread = jnp.mean(centre * centre, axis=-1, keepdims=True)
    return centre * lax.rsqrt(spread + 1e-05) * gain + offset


def gelu_tanh(values):
    return jax.nn.gelu(values, approximate=True)


def contract(left, right, dims):
    return lax.dot_general(left, right, (dims, ((), ())), preferred_element_type=f32)


def tile_visible(length, part):
    shape = ((part + 1) * PART, PART)
    key_place = lax.broadcasted_iota(jnp.int32, shape, 0)
    query_place = lax.broadcasted_iota(jnp.int32, shape, 1) + part * PART
    return (key_place <= query_place) & (key_place < length)


def place_pieces(here, pieces, shelf, whole):
    span = pieces[0].shape[1]
    for step, piece in enumerate(pieces):
        shelf[here ^ step] = piece[...]
    for at in range(len(pieces)):
        whole[:, at * span : (at + 1) * span] = shelf[at]


def hand_out(here, whole, shelf, pieces):
    span = pieces[0].shape[1]
    for at in range(len(pieces)):
        shelf[at] = whole[:, at * span : (at + 1) * span]
    for step, piece in enumerate(pieces):
        piece[...] = shelf[here ^ step]


def turned(rows):
    return rows.astype(f32).T.astype(bf16)


def forward_kernel(groups, lengths, here, *refs):
    pieces, refs = refs[:groups], refs[groups:]
    packed, mixed, totals = refs[:3]
    outs, refs = refs[3 : 3 + groups], refs[3 + groups :]
    shelf, out_shelf, key_rows = refs
    place_pieces(here[0], pieces, shelf, packed)
    key_rows[...] = turned(packed[HEAD : 2 * HEAD, :])
    for query_index in range(PASSES):
        for part in range(PASS_SLOTS // PART):
            query_at = query_index * PASS_SLOTS + part * PART
            query_span = slice(query_at, query_at + PART)
            queries = packed[:HEAD, query_span] * jnp.asarray(0.125, bf16)
            top = jnp.full((1, PART), masked_value, f32)
            total = jnp.zeros((1, PART), f32)
            acc = jnp.zeros((HEAD, PART), f32)
            for key_index in range(query_index + 1):
                key_at = key_index * PASS_SLOTS
                key_span = slice(key_at, key_at + (part + 1) * PART)
                scores = contract(key_rows[key_span, :], queries, ((1,), (0,)))
                shown = tile_visible(lengths[0, key_index], part)
                scores = jnp.where(shown, scores, masked_value)
                newest = jnp.maximum(top, jnp.max(scores, axis=0, keepdims=True))
                shares = jnp.exp(scores - newest)
                fade = jnp.exp(top - newest)
                total = total * fade + jnp.sum(shares, axis=0, keepdims=True)
                values = packed[2 * HEAD :, key_span]
                acc = acc * fade + contract(values, shares.astype(bf16), ((1,), (0,)))
                top = newest
            mixed[:, query_span] = (acc / total).astype(bf16)
            place = slice(part * PART, (part + 1) * PART)
            totals[query_index : query_index + 1, place] = top + jnp.log(total)
    hand_out(here[0], mixed, out_shelf, outs)


def backward_kernel(groups, lengths, here, packed, mixed, totals, *refs):
    pieces, refs = refs[:groups], refs[groups:]
    outs, refs = refs[:groups], refs[groups:]
    shelf, out_shelf, grad, rows, grad_rows, grad_query, result = refs
    place_pieces(here[0], pieces, shelf, grad)
    rows[...] = turned(packed[...])
    grad_rows[...] = turned(grad[...])
    grad_query[...] = jnp.zeros_like(grad_query)
    eighth = jnp.asarray(0.125, bf16)
    parts = PASS_SLOTS // PART

    def key_pass(key_index, _):
        key_at = pl.multiple_of(key_index * PASS_SLOTS, PASS_SLOTS)
        key_span = pl.ds(key_at, PASS_SLOTS)
        keys = rows[key_span, HEAD : 2 * HEAD] * eighth
        keys_turned = packed[HEAD : 2 * HEAD, key_span] * eighth
        values = rows[key_span, 2 * HEAD :]
        length = lengths[0, key_index]

        def query_pass(query_index, carried):
            carried = list(carried)
            for part in range(parts):
                seen = (part + 1) * PART
                start = query_index * PASS_SLOTS + part * PART
                query_span = pl.ds(pl.multiple_of(start, PART), PART)
                place = slice(part * PART, seen)
                grads = grad[:, query_span]
                product = grads.astype(f32) * mixed[:, query_span].astype(f32)
                delta = jnp.sum(product, axis=0, keepdims=True)
                scores = contract(keys[:seen], packed[:HEAD, query_span], ((1,), (0,)))
                shares = jnp.exp(scores - totals[pl.ds(query_index, 1), place])
                shares = jnp.where(tile_visible(length, part), shares, 0.0)
                grad_shares = contract(values[:seen], grads, ((1,), (0,)))
                grad_scores = (shares * (grad_shares - delta)).astype(bf16)
                add_query = contract(keys_turned[:, :seen], grad_scores, ((1,), (0,)))
                grad_query[:, query_span] += add_query
                add_value = contract(shares.astype(bf16), grad_rows[query_span, :], ((1,), (0,)))
                queries = rows[query_span, :HEAD] * eighth
                add_key = contract(grad_scores, queries, ((1,), (0,)))
                for n in range(part + 1):
                    block = slice(n * PART, (n + 1) * PART)
                    carried[n] += add_key[block]
                    carried[parts + n] += add_value[block]
            return tuple(carried)

        empty = jnp.zeros((PART, HEAD), f32)
        found = lax.fori_loop(key_index, PASSES, query_pass, (empty,) * (2 * parts))
        grad_key = jnp.concatenate(found[:parts], axis=0)
        grad_value = jnp.concatenate(found[parts:], axis=0)
        result[HEAD : 2 * HEAD, key_span] = grad_key.T.astype(bf16)
        result[2 * HEAD :, key_span] = grad_value.T.astype(bf16)
        return 0

    lax.fori_loop(0, PASSES, key_pass, 0)
    result[:HEAD, :] = grad_query[...].astype(bf16)
    hand_out(here[0], result, out_shelf, outs)


in_vmem = functools.partial(pl.BlockSpec, memory_space=pltpu.VMEM)
in_smem = functools.partial(pl.BlockSpec, memory_space=pltpu.SMEM)


def attend(lengths, here, pieces):
    groups = len(pieces)
    triple, span = pieces[0].shape
    slots = span * groups
    return pl.pallas_call(
        functools.partial(forward_kernel, groups),
        out_shape=[
            jax.ShapeDtypeStruct((triple, slots), bf16),
            jax.ShapeDtypeStruct((HEAD, slots), bf16),
            jax.ShapeDtypeStruct((PASSES, PASS_SLOTS), f32),
        ]
        + [jax.ShapeDtypeStruct((HEAD, span), bf16)] * groups,
        in_specs=[in_smem(), in_smem()] + [in_vmem()] * groups,
        out_specs=[in_vmem()] * (3 + groups),
        scratch_shapes=[
            pltpu.VMEM((groups, triple, span), bf16),
            pltpu.VMEM((groups, HEAD, span), bf16),
            pltpu.VMEM((slots, HEAD), bf16),
        ],
        compiler_params=pltpu.CompilerParams(vmem_limit_bytes=32 << 20),
        cost_estimate=pl.CostEstimate(flops=10**10, transcendentals=0, bytes_accessed=10**6),
        name="attend",
    )(lengths, here, *pieces)


def attend_back(lengths, here, packed, mixed, totals, pieces):
    groups = len(pieces)
    triple, slots = packed.shape
    span = slots // groups
    return pl.pallas_call(
        functools.partial(backward_kernel, groups),
        out_shape=[jax.ShapeDtypeStruct((triple, span), bf16)] * groups,
        in_specs=[in_smem(), in_smem()] + [in_vmem()] * (3 + groups),
        out_specs=[in_vmem()] * groups,
        scratch_shapes=[
            pltpu.VMEM((groups, HEAD, span), bf16),
            pltpu.VMEM((groups, triple, span), bf16),
            pltpu.VMEM((HEAD, slots), bf16),
            pltpu.VMEM((slots, triple), bf16),
            pltpu.VMEM((slots, HEAD), bf16),
            pltpu.VMEM((HEAD, slots), f32),
            pltpu.VMEM((triple, slots), bf16),
        ],
        compiler_params=pltpu.CompilerParams(vmem_limit_bytes=32 << 20),
        cost_estimate=pl.CostEstimate(
            flops=15 * 10**9, transcendentals=0, bytes_accessed=10**6
        ),
        name="attend_back",
    )(lengths, here, packed, mixed, totals, *pieces)


def row_major(values):
    return with_layout_constraint(values, Layout(tuple(range(values.ndim))))


def after(values, *others):
    return lax.optimization_barrier((values, others))[0]


def swap_with(values, axis, step):
    size = lax.axis_size(axis)
    return lax.ppermute(values, axis, [(i, i ^ step) for i in range(size)])


def axis_bits(axis):
    size = lax.axis_size(axis)
    assert size & (size - 1) == 0
    return [(axis, 1 << n) for n in reversed(range(size.bit_length() - 1))]


def bit_order(flip):
    places = axis_bits("seq") + axis_bits("blk")
    near = axis_bits("seq")
    far = near[:-1][::-1] if flip else near[:-1]
    return places, axis_bits("blk") + far + near[-1:]


def own_bit(bit):
    return (lax.axis_index(bit[0]) & bit[1]) != 0


class Gather:
    def __init__(self, piece, flip):
        self.places, self.order = bit_order(flip)
        self.shape = piece.shape
        self.piece = piece
        self.done = []

    def grow(self, count=None):
        count = len(self.order) if count is None else count
        for bit in self.order[:count]:
            other = swap_with(self.piece, *bit)
            self.done = sorted(self.done + [bit], key=self.places.index)
            mine = own_bit(bit)
            low = jnp.where(mine, other, self.piece)
            high = jnp.where(mine, self.piece, other)
            self.piece = jnp.stack([low, high], axis=self.done.index(bit))
        self.order = self.order[count:]
        return self.piece

    def whole(self):
        return self.grow().reshape((-1,) + self.shape[1:])


class Scatter:
    def __init__(self, whole, flip):
        self.left, order = bit_order(flip)
        self.order = order[::-1]
        self.sent = None
        rows = whole.shape[0] >> len(order)
        self.piece = whole.reshape((2,) * len(order) + (rows,) + whole.shape[1:])

    def send(self):
        bit, self.order = self.order[0], self.order[1:]
        at = self.left.index(bit)
        self.left = [place for place in self.left if place != bit]
        low = lax.index_in_dim(self.piece, 0, at, keepdims=False)
        high = lax.index_in_dim(self.piece, 1, at, keepdims=False)
        mine = own_bit(bit)
        self.bit = bit
        self.sent = jnp.where(mine, low, high)
        self.kept = jnp.where(mine, high, low)
        return (self.sent, self.kept)

    def receive(self, *others):
        if self.sent is None:
            return
        other = after(swap_with(self.sent, *self.bit), others)
        self.sent = None
        self.piece = (self.kept.astype(f32) + other.astype(f32)).astype(bf16)

    def finish(self):
        self.receive()
        while self.order:
            self.send()
            self.receive()
        return self.piece


def swap_pieces(pieces):
    return [swap_with(piece, "blk", step) if step else piece for step, piece in enumerate(pieces)]


def in_order(pieces):
    here = lax.axis_index("blk")
    result = jnp.zeros((len(pieces),) + pieces[0].shape, pieces[0].dtype)
    for step, piece in enumerate(pieces):
        result = lax.dynamic_update_index_in_dim(result, piece, here ^ step, 0)
    return result


def at_group(values, group):
    return lax.dynamic_index_in_dim(values, group, 0, keepdims=False)


def by_head(rows, groups):
    count = rows.shape[0]
    return rows.reshape(count, 3, groups, -1, HEAD).transpose(0, 3, 2, 1, 4).reshape(count, -1)


def by_kind(rows, groups):
    count = rows.shape[0]
    return rows.reshape(count, -1, groups, 3, HEAD).transpose(0, 3, 2, 1, 4).reshape(count, -1)


def norm_parts(values):
    centre = values - jnp.mean(values, axis=-1, keepdims=True)
    spread = jnp.mean(centre * centre, axis=-1, keepdims=True)
    scale = lax.rsqrt(spread + 1e-05)
    return centre * scale, scale


def norm_back(values, gain, grad):
    hat, scale = norm_parts(values)
    edge = grad * gain
    part = scale * (
        edge
        - jnp.mean(edge, axis=-1, keepdims=True)
        - hat * jnp.mean(edge * hat, axis=-1, keepdims=True)
    )
    return part, jnp.sum(grad * hat, axis=0), jnp.sum(grad, axis=0)


def on_device(states, cotangent, lengths, w_qkv, w_out, w_up, w_down, vectors, up_bias):
    _, row_count, width = states.shape
    groups = lax.axis_size("blk")
    own = w_qkv.shape[0]
    wide = w_up.shape[1]
    ratio = wide // width
    vector_count = vectors.shape[0]
    heads = width // HEAD // groups
    span = 3 * HEAD
    small = vector_count + ratio

    here = lax.axis_index("blk").astype(jnp.int32)
    parts = by_head(w_qkv, groups)
    middle_column = parts.shape[1] // 2
    extra = [vectors.T, up_bias.reshape(own, ratio), jnp.zeros((own, -small % 128), bf16)]
    streams = [
        Gather(jnp.concatenate([parts[:, :middle_column]] + extra, axis=1), False),
        Gather(parts[:, middle_column:], True),
    ]
    blk_steps = len(axis_bits("blk"))
    begun = [stream.grow(blk_steps) for stream in streams]
    w_out, w_up, w_down = after((w_out, w_up, w_down), begun)
    later = [Gather(w_up, False), Gather(w_down, True), Gather(w_out, False)]
    for one in later:
        one.grow(blk_steps)
    first = [stream.whole() for stream in streams]
    for one in later:
        one.piece = after(one.piece, first)
        one.grow(1)
    full_qkv = jnp.concatenate([first[0][:, :middle_column], first[1]], axis=1)
    head_qkv = [full_qkv[:, h * groups * span : (h + 1) * groups * span] for h in range(heads)]
    corner = first[0][:, middle_column : middle_column + small]
    table = corner[:, :vector_count].astype(f32).T
    bias_up = corner[:, vector_count:].astype(f32).reshape(wide)

    slots = lax.axis_index("blk") * row_count + jnp.arange(row_count, dtype=jnp.int32)
    pass_of = (slots // PASS_SLOTS)[:, None] == jnp.arange(PASSES, dtype=jnp.int32)[None, :]
    bounds = jnp.sum(jnp.where(pass_of, lengths[0][None, :], 0), axis=1)
    live = (slots % PASS_SLOTS < bounds).astype(f32)[:, None]

    added = jnp.zeros((row_count, width), f32)
    for index in range(PASSES):
        added = jnp.where(pass_of[:, index : index + 1], table[index], added)
    start = states[0].astype(f32) + added
    normed_a = layer_norm(start, table[5], table[6]).astype(bf16)
    column = jnp.arange(3 * width, dtype=jnp.int32)
    kind = column // HEAD % 3
    source = (column // span % groups) * heads + column // (span * groups)
    source = source * HEAD + column % HEAD
    match = source[:, None] == jnp.arange(width, dtype=jnp.int32)[None, :]
    choice = jnp.where((kind == 0)[:, None], table[7], jnp.where((kind == 2)[:, None], table[8], 0.0))
    bias_three = jnp.sum(jnp.where(match, choice, 0.0), axis=1, keepdims=True)
    bias_three = bias_three.reshape(heads, -1, 1)
    sending = []
    for h in range(heads):
        rows = contract(head_qkv[h], normed_a, ((0,), (1,))) + bias_three[h]
        rows = rows.astype(bf16).reshape(groups, span, row_count)
        sending.append([row_major(at_group(rows, here ^ step)) for step in range(groups)])
    for one in later:
        one.piece = after(one.piece, sending[0])
    kept = []
    arrived = []
    returned = []
    for h in range(heads):
        pieces = swap_pieces(after(sending[h], arrived))
        arrived = pieces
        if h == 1:
            pieces = after(pieces, [one.piece for one in later])
        packed, mixed, totals, *pieces = attend(lengths, here[None], pieces)
        kept.append((packed, mixed, totals))
        returned.append(swap_pieces(pieces))
    full_up, full_down, full_out = [one.whole() for one in later]
    returned[:-1] = after(returned[:-1], pieces)
    returned = [in_order(pieces) for pieces in returned]
    heads_out = jnp.stack(returned, axis=1).reshape(width, row_count)
    middle = start + live * (contract(heads_out, full_out, ((0,), (0,))) + table[9])
    normed_b = layer_norm(middle, table[10], table[11]).astype(bf16)
    up_sum = contract(normed_b, full_up, ((1,), (0,))) + bias_up
    activated, gelu_pull = jax.vjp(gelu_tanh, up_sum)
    hidden = activated.astype(bf16)
    outcome = middle + live * (contract(hidden, full_down, ((1,), (0,))) + table[12])
    incoming = cotangent[0].astype(f32)
    grad_branch = (live * incoming).astype(bf16)
    grad_hidden = contract(grad_branch, full_down, ((1,), (1,)))
    grad_upsum = gelu_pull(grad_hidden)[0].astype(bf16)
    grad_normb = contract(grad_upsum, full_up, ((1,), (1,)))
    middle_part, gain_grad_b, shift_grad_b = norm_back(middle, table[10], grad_normb)
    grad_middle = incoming + middle_part
    grad_attn = (live * grad_middle).astype(bf16)
    grad_heads = contract(full_out, grad_attn, ((1,), (1,))).astype(bf16)
    grad_heads = grad_heads.reshape(groups, heads, HEAD, row_count)
    sending = [
        [row_major(at_group(grad_heads[:, h], here ^ step)) for step in range(groups)]
        for h in range(heads)
    ]
    arrived = []
    late = []
    parts = []
    for h in range(heads):
        pieces = swap_pieces(after(sending[h], arrived))
        arrived = pieces
        if h == 0:
            pieces = after(pieces, outcome)
        if not late:
            hidden_late, grad_branch_late, grad_upsum_late, grad_attn_late = after(
                (hidden, grad_branch, grad_upsum, grad_attn), sending
            )
            grad_down = contract(hidden_late, grad_branch_late, ((0,), (0,))).astype(bf16)
            grad_up = contract(normed_b, grad_upsum_late, ((0,), (0,))).astype(bf16)
            grad_out = contract(heads_out, grad_attn_late, ((1,), (0,))).astype(bf16)
            grad_up = jnp.concatenate([grad_up, grad_out], axis=1)
            late = [Scatter(grad_down, True), Scatter(grad_up, False)]
        else:
            for one in late:
                one.receive(parts[-1])
        pieces = after(pieces, [one.send() for one in late])
        back = attend_back(lengths, here[None], *kept[h], pieces)
        parts.append(back)
    grad_projected = []
    for back in parts:
        grad_projected.append(swap_pieces(back))
    grad_projected[:-1] = after(grad_projected[:-1], parts[-1])
    for one in late:
        one.receive(parts[-1])
    sent = [one.send() for one in late]

    whole = [in_order(pieces).reshape(groups * span, row_count) for pieces in grad_projected[:-1]]
    early = [row_major(contract(normed_a, part, ((0,), (1,))).astype(bf16)) for part in whole]
    early = Scatter(after(jnp.concatenate(early, axis=1), sent), True)
    pieces = after(grad_projected[-1], early.send())
    whole.append(in_order(pieces).reshape(groups * span, row_count))
    final = row_major(contract(normed_a, whole[-1], ((0,), (1,))).astype(bf16))
    grad_norma = sum(contract(part, weights, ((0,), (1,))) for part, weights in zip(whole, head_qkv))
    started = early.sent
    early.receive(whole[-1])
    sent = [early.send()]
    for one in late:
        one.receive(started)
        sent.append(one.send())
    grad_norma = after(grad_norma, sent)
    sums = [jnp.sum(part.astype(f32), axis=1) for part in whole]
    column_sums = by_kind(jnp.concatenate(sums)[None], groups)[0]
    start_part, gain_grad_a, shift_grad_a = norm_back(start, table[5], grad_norma)
    grad_start = grad_middle + start_part
    grad_embed = [
        jnp.sum(jnp.where(pass_of[:, index : index + 1], grad_start, 0.0), axis=0)
        for index in range(PASSES)
    ]
    vector_grads = jnp.stack(
        grad_embed
        + [
            gain_grad_a,
            shift_grad_a,
            column_sums[:width],
            column_sums[2 * width :],
            jnp.sum(grad_attn.astype(f32), axis=0),
            gain_grad_b,
            shift_grad_b,
            jnp.sum(grad_branch.astype(f32), axis=0),
        ]
    )
    bias_grads = jnp.sum(grad_upsum.astype(f32), axis=0)
    extra = [vector_grads.T.astype(bf16), bias_grads.reshape(width, ratio).astype(bf16)]
    last = Scatter(jnp.concatenate([final] + extra + [jnp.zeros((width, -small % 128), bf16)], axis=1), False)
    wave = 0
    tied = last.send()
    early.receive(tied)
    while last.order:
        sent = [early.send()] if early.order else []
        if wave % 2 == 0 and late[0].order:
            for one in late:
                one.receive(tied)
                sent.append(one.send())
        elif not late[0].order:
            for one in late:
                one.receive(tied)
                sent.append(one.piece)
        last.receive(sent)
        tied = last.send()
        early.receive(tied)
        wave += 1
    last.receive()
    for one in late:
        one.receive(tied)
        one.finish()
    grad_down = late[0].piece
    grad_up = late[1].piece[:, :wide]
    grad_out = late[1].piece[:, wide:]
    grad_qkv = [early.finish(), last.piece[:, : groups * span]]
    extra = last.piece[:, groups * span :].astype(f32)
    return (
        outcome.astype(bf16)[None],
        grad_start.astype(bf16)[None],
        by_kind(jnp.concatenate(grad_qkv, axis=1).astype(f32), groups),
        grad_out.astype(f32),
        grad_up.astype(f32),
        grad_down.astype(f32),
        extra[:, :vector_count].T,
        extra[:, vector_count:small].reshape(own * ratio),
    )


def solution(mesh):
    split = P(both, None)
    return jax.shard_map(
        on_device,
        mesh=mesh,
        in_specs=(
            P("seq", "blk", None),
            P("seq", "blk", None),
            P("seq", None),
            split,
            split,
            split,
            split,
            P(None, both),
            P(both),
        ),
        out_specs=(
            P("seq", "blk", None),
            P("seq", "blk", None),
            split,
            split,
            split,
            split,
            P(None, both),
            P(both),
        ),
        check_vma=False,
    )
```

```python
import functools

import jax
import jax.numpy as jnp
from jax import lax
from jax.experimental import pallas as pl
from jax.experimental.layout import Layout, with_layout_constraint
from jax.experimental.pallas import tpu as pltpu
from jax.sharding import PartitionSpec as P


HEAD = 64
PASSES = 5
PASS_SLOTS = 512


masked_value = -1e30
both = ("seq", "blk")
f32 = jnp.float32
bf16 = jnp.bfloat16


def layer_norm(values, gain, offset):
    centre = values - jnp.mean(values, axis=-1, keepdims=True)
    spread = jnp.mean(centre * centre, axis=-1, keepdims=True)
    return centre * lax.rsqrt(spread + 1e-05) * gain + offset


def gelu_tanh(values):
    return jax.nn.gelu(values, approximate=True)


def contract(left, right, dims):
    return lax.dot_general(left, right, (dims, ((), ())), preferred_element_type=f32)


def tile_visible(length):
    key_place = lax.broadcasted_iota(jnp.int32, (PASS_SLOTS, PASS_SLOTS), 0)
    query_place = lax.broadcasted_iota(jnp.int32, (PASS_SLOTS, PASS_SLOTS), 1)
    return (key_place <= query_place) & (key_place < length)


def place_pieces(here, pieces, shelf, whole):
    span = pieces[0].shape[1]
    for step, piece in enumerate(pieces):
        shelf[here ^ step] = piece[...]
    for at in range(len(pieces)):
        whole[:, at * span : (at + 1) * span] = shelf[at]


def hand_out(here, whole, shelf, pieces):
    span = pieces[0].shape[1]
    for at in range(len(pieces)):
        shelf[at] = whole[:, at * span : (at + 1) * span]
    for step, piece in enumerate(pieces):
        piece[...] = shelf[here ^ step]


def turned(rows):
    return rows.astype(f32).T.astype(bf16)


def forward_kernel(groups, lengths, here, *refs):
    pieces, refs = refs[:groups], refs[groups:]
    packed, mixed, totals = refs[:3]
    outs, refs = refs[3 : 3 + groups], refs[3 + groups :]
    shelf, out_shelf, key_rows = refs
    place_pieces(here[0], pieces, shelf, packed)
    key_rows[...] = turned(packed[HEAD : 2 * HEAD, :])
    for query_index in range(PASSES):
        query_span = slice(query_index * PASS_SLOTS, (query_index + 1) * PASS_SLOTS)
        queries = packed[:HEAD, query_span] * jnp.asarray(0.125, bf16)
        top = jnp.full((1, PASS_SLOTS), masked_value, f32)
        total = jnp.zeros((1, PASS_SLOTS), f32)
        acc = jnp.zeros((HEAD, PASS_SLOTS), f32)
        for key_index in range(query_index + 1):
            key_span = slice(key_index * PASS_SLOTS, (key_index + 1) * PASS_SLOTS)
            scores = contract(key_rows[key_span, :], queries, ((1,), (0,)))
            scores = jnp.where(tile_visible(lengths[0, key_index]), scores, masked_value)
            newest = jnp.maximum(top, jnp.max(scores, axis=0, keepdims=True))
            shares = jnp.exp(scores - newest)
            fade = jnp.exp(top - newest)
            total = total * fade + jnp.sum(shares, axis=0, keepdims=True)
            values = packed[2 * HEAD :, key_span]
            acc = acc * fade + contract(values, shares.astype(bf16), ((1,), (0,)))
            top = newest
        mixed[:, query_span] = (acc / total).astype(bf16)
        totals[query_index : query_index + 1, :] = top + jnp.log(total)
    hand_out(here[0], mixed, out_shelf, outs)


def backward_kernel(groups, lengths, here, packed, mixed, totals, *refs):
    pieces, refs = refs[:groups], refs[groups:]
    outs, refs = refs[:groups], refs[groups:]
    shelf, out_shelf, grad, rows, grad_rows, grad_query, result = refs
    place_pieces(here[0], pieces, shelf, grad)
    rows[...] = turned(packed[...])
    grad_rows[...] = turned(grad[...])
    grad_query[...] = jnp.zeros_like(grad_query)
    eighth = jnp.asarray(0.125, bf16)

    def key_pass(key_index, _):
        key_at = pl.multiple_of(key_index * PASS_SLOTS, PASS_SLOTS)
        key_span = pl.ds(key_at, PASS_SLOTS)
        keys = rows[key_span, HEAD : 2 * HEAD] * eighth
        keys_turned = packed[HEAD : 2 * HEAD, key_span] * eighth
        values = rows[key_span, 2 * HEAD :]
        shown = tile_visible(lengths[0, key_index])

        def query_pass(query_index, carried):
            grad_key, grad_value = carried
            query_at = pl.multiple_of(query_index * PASS_SLOTS, PASS_SLOTS)
            query_span = pl.ds(query_at, PASS_SLOTS)
            grads = grad[:, query_span]
            product = grads.astype(f32) * mixed[:, query_span].astype(f32)
            delta = jnp.sum(product, axis=0, keepdims=True)
            scores = contract(keys, packed[:HEAD, query_span], ((1,), (0,)))
            shares = jnp.exp(scores - totals[pl.ds(query_index, 1), :])
            shares = jnp.where(shown, shares, 0.0)
            grad_shares = contract(values, grads, ((1,), (0,)))
            grad_scores = (shares * (grad_shares - delta)).astype(bf16)
            grad_query[:, query_span] += contract(keys_turned, grad_scores, ((1,), (0,)))
            grad_value += contract(shares.astype(bf16), grad_rows[query_span, :], ((1,), (0,)))
            queries = rows[query_span, :HEAD] * eighth
            grad_key += contract(grad_scores, queries, ((1,), (0,)))
            return grad_key, grad_value

        empty = jnp.zeros((PASS_SLOTS, HEAD), f32)
        grad_key, grad_value = lax.fori_loop(key_index, PASSES, query_pass, (empty, empty))
        result[HEAD : 2 * HEAD, key_span] = grad_key.T.astype(bf16)
        result[2 * HEAD :, key_span] = grad_value.T.astype(bf16)
        return 0

    lax.fori_loop(0, PASSES, key_pass, 0)
    result[:HEAD, :] = grad_query[...].astype(bf16)
    hand_out(here[0], result, out_shelf, outs)


in_vmem = functools.partial(pl.BlockSpec, memory_space=pltpu.VMEM)
in_smem = functools.partial(pl.BlockSpec, memory_space=pltpu.SMEM)


def attend(lengths, here, pieces):
    groups = len(pieces)
    triple, span = pieces[0].shape
    slots = span * groups
    return pl.pallas_call(
        functools.partial(forward_kernel, groups),
        out_shape=[
            jax.ShapeDtypeStruct((triple, slots), bf16),
            jax.ShapeDtypeStruct((HEAD, slots), bf16),
            jax.ShapeDtypeStruct((PASSES, PASS_SLOTS), f32),
        ]
        + [jax.ShapeDtypeStruct((HEAD, span), bf16)] * groups,
        in_specs=[in_smem(), in_smem()] + [in_vmem()] * groups,
        out_specs=[in_vmem()] * (3 + groups),
        scratch_shapes=[
            pltpu.VMEM((groups, triple, span), bf16),
            pltpu.VMEM((groups, HEAD, span), bf16),
            pltpu.VMEM((slots, HEAD), bf16),
        ],
        compiler_params=pltpu.CompilerParams(vmem_limit_bytes=32 << 20),
        cost_estimate=pl.CostEstimate(flops=10**10, transcendentals=0, bytes_accessed=10**6),
        name="attend",
    )(lengths, here, *pieces)


def attend_back(lengths, here, packed, mixed, totals, pieces):
    groups = len(pieces)
    triple, slots = packed.shape
    span = slots // groups
    return pl.pallas_call(
        functools.partial(backward_kernel, groups),
        out_shape=[jax.ShapeDtypeStruct((triple, span), bf16)] * groups,
        in_specs=[in_smem(), in_smem()] + [in_vmem()] * (3 + groups),
        out_specs=[in_vmem()] * groups,
        scratch_shapes=[
            pltpu.VMEM((groups, HEAD, span), bf16),
            pltpu.VMEM((groups, triple, span), bf16),
            pltpu.VMEM((HEAD, slots), bf16),
            pltpu.VMEM((slots, triple), bf16),
            pltpu.VMEM((slots, HEAD), bf16),
            pltpu.VMEM((HEAD, slots), f32),
            pltpu.VMEM((triple, slots), bf16),
        ],
        compiler_params=pltpu.CompilerParams(vmem_limit_bytes=32 << 20),
        cost_estimate=pl.CostEstimate(
            flops=15 * 10**9, transcendentals=0, bytes_accessed=10**6
        ),
        name="attend_back",
    )(lengths, here, packed, mixed, totals, *pieces)


def row_major(values):
    return with_layout_constraint(values, Layout(tuple(range(values.ndim))))


def after(values, *others):
    return lax.optimization_barrier((values, others))[0]


def swap_with(values, axis, step):
    size = lax.axis_size(axis)
    return lax.ppermute(values, axis, [(i, i ^ step) for i in range(size)])


def axis_bits(axis):
    size = lax.axis_size(axis)
    assert size & (size - 1) == 0
    return [(axis, 1 << n) for n in reversed(range(size.bit_length() - 1))]


def bit_order(flip):
    places = axis_bits("seq") + axis_bits("blk")
    near = axis_bits("seq")
    far = near[:-1][::-1] if flip else near[:-1]
    return places, axis_bits("blk") + far + near[-1:]


def own_bit(bit):
    return (lax.axis_index(bit[0]) & bit[1]) != 0


class Gather:
    def __init__(self, piece, flip):
        self.places, self.order = bit_order(flip)
        self.shape = piece.shape
        self.piece = piece
        self.done = []

    def grow(self, count=None):
        count = len(self.order) if count is None else count
        for bit in self.order[:count]:
            other = swap_with(self.piece, *bit)
            self.done = sorted(self.done + [bit], key=self.places.index)
            mine = own_bit(bit)
            low = jnp.where(mine, other, self.piece)
            high = jnp.where(mine, self.piece, other)
            self.piece = jnp.stack([low, high], axis=self.done.index(bit))
        self.order = self.order[count:]
        return self.piece

    def whole(self):
        return self.grow().reshape((-1,) + self.shape[1:])


class Scatter:
    def __init__(self, whole, flip):
        self.left, order = bit_order(flip)
        self.order = order[::-1]
        self.sent = None
        rows = whole.shape[0] >> len(order)
        self.piece = whole.reshape((2,) * len(order) + (rows,) + whole.shape[1:])

    def send(self):
        bit, self.order = self.order[0], self.order[1:]
        at = self.left.index(bit)
        self.left = [place for place in self.left if place != bit]
        low = lax.index_in_dim(self.piece, 0, at, keepdims=False)
        high = lax.index_in_dim(self.piece, 1, at, keepdims=False)
        mine = own_bit(bit)
        self.bit = bit
        self.sent = jnp.where(mine, low, high)
        self.kept = jnp.where(mine, high, low)
        return (self.sent, self.kept)

    def receive(self, *others):
        if self.sent is None:
            return
        other = after(swap_with(self.sent, *self.bit), others)
        self.sent = None
        self.piece = (self.kept.astype(f32) + other.astype(f32)).astype(bf16)

    def finish(self):
        self.receive()
        while self.order:
            self.send()
            self.receive()
        return self.piece


def swap_pieces(pieces):
    return [swap_with(piece, "blk", step) if step else piece for step, piece in enumerate(pieces)]


def in_order(pieces):
    here = lax.axis_index("blk")
    result = jnp.zeros((len(pieces),) + pieces[0].shape, pieces[0].dtype)
    for step, piece in enumerate(pieces):
        result = lax.dynamic_update_index_in_dim(result, piece, here ^ step, 0)
    return result


def at_group(values, group):
    return lax.dynamic_index_in_dim(values, group, 0, keepdims=False)


def by_head(rows, groups):
    count = rows.shape[0]
    return rows.reshape(count, 3, groups, -1, HEAD).transpose(0, 3, 2, 1, 4).reshape(count, -1)


def by_kind(rows, groups):
    count = rows.shape[0]
    return rows.reshape(count, -1, groups, 3, HEAD).transpose(0, 3, 2, 1, 4).reshape(count, -1)


def norm_parts(values):
    centre = values - jnp.mean(values, axis=-1, keepdims=True)
    spread = jnp.mean(centre * centre, axis=-1, keepdims=True)
    scale = lax.rsqrt(spread + 1e-05)
    return centre * scale, scale


def norm_back(values, gain, grad):
    hat, scale = norm_parts(values)
    edge = grad * gain
    part = scale * (
        edge
        - jnp.mean(edge, axis=-1, keepdims=True)
        - hat * jnp.mean(edge * hat, axis=-1, keepdims=True)
    )
    return part, jnp.sum(grad * hat, axis=0), jnp.sum(grad, axis=0)


def on_device(states, cotangent, lengths, w_qkv, w_out, w_up, w_down, vectors, up_bias):
    _, row_count, width = states.shape
    groups = lax.axis_size("blk")
    own = w_qkv.shape[0]
    wide = w_up.shape[1]
    ratio = wide // width
    vector_count = vectors.shape[0]
    heads = width // HEAD // groups
    span = 3 * HEAD
    small = vector_count + ratio

    here = lax.axis_index("blk").astype(jnp.int32)
    parts = by_head(w_qkv, groups)
    middle_column = parts.shape[1] // 2
    extra = [vectors.T, up_bias.reshape(own, ratio), jnp.zeros((own, -small % 128), bf16)]
    streams = [
        Gather(jnp.concatenate([parts[:, :middle_column]] + extra, axis=1), False),
        Gather(parts[:, middle_column:], True),
    ]
    blk_steps = len(axis_bits("blk"))
    begun = [stream.grow(blk_steps) for stream in streams]
    w_out, w_up, w_down = after((w_out, w_up, w_down), begun)
    later = [Gather(w_up, False), Gather(w_down, True), Gather(w_out, False)]
    for one in later:
        one.grow(blk_steps)
    first = [stream.whole() for stream in streams]
    for one in later:
        one.piece = after(one.piece, first)
        one.grow(1)
    full_qkv = jnp.concatenate([first[0][:, :middle_column], first[1]], axis=1)
    head_qkv = [full_qkv[:, h * groups * span : (h + 1) * groups * span] for h in range(heads)]
    corner = first[0][:, middle_column : middle_column + small]
    table = corner[:, :vector_count].astype(f32).T
    bias_up = corner[:, vector_count:].astype(f32).reshape(wide)

    slots = lax.axis_index("blk") * row_count + jnp.arange(row_count, dtype=jnp.int32)
    pass_of = (slots // PASS_SLOTS)[:, None] == jnp.arange(PASSES, dtype=jnp.int32)[None, :]
    bounds = jnp.sum(jnp.where(pass_of, lengths[0][None, :], 0), axis=1)
    live = (slots % PASS_SLOTS < bounds).astype(f32)[:, None]

    added = jnp.zeros((row_count, width), f32)
    for index in range(PASSES):
        added = jnp.where(pass_of[:, index : index + 1], table[index], added)
    start = states[0].astype(f32) + added
    normed_a = layer_norm(start, table[5], table[6]).astype(bf16)
    column = jnp.arange(3 * width, dtype=jnp.int32)
    kind = column // HEAD % 3
    source = (column // span % groups) * heads + column // (span * groups)
    source = source * HEAD + column % HEAD
    match = source[:, None] == jnp.arange(width, dtype=jnp.int32)[None, :]
    choice = jnp.where((kind == 0)[:, None], table[7], jnp.where((kind == 2)[:, None], table[8], 0.0))
    bias_three = jnp.sum(jnp.where(match, choice, 0.0), axis=1, keepdims=True)
    bias_three = bias_three.reshape(heads, -1, 1)
    sending = []
    for h in range(heads):
        rows = contract(head_qkv[h], normed_a, ((0,), (1,))) + bias_three[h]
        rows = rows.astype(bf16).reshape(groups, span, row_count)
        sending.append([row_major(at_group(rows, here ^ step)) for step in range(groups)])
    for one in later:
        one.piece = after(one.piece, sending[0])
    kept = []
    arrived = []
    returned = []
    for h in range(heads):
        pieces = swap_pieces(after(sending[h], arrived))
        arrived = pieces
        if h == 1:
            pieces = after(pieces, [one.piece for one in later])
        packed, mixed, totals, *pieces = attend(lengths, here[None], pieces)
        kept.append((packed, mixed, totals))
        returned.append(swap_pieces(pieces))
    full_up, full_down, full_out = [one.whole() for one in later]
    returned[:-1] = after(returned[:-1], pieces)
    returned = [in_order(pieces) for pieces in returned]
    heads_out = jnp.stack(returned, axis=1).reshape(width, row_count)
    middle = start + live * (contract(heads_out, full_out, ((0,), (0,))) + table[9])
    normed_b = layer_norm(middle, table[10], table[11]).astype(bf16)
    up_sum = contract(normed_b, full_up, ((1,), (0,))) + bias_up
    activated, gelu_pull = jax.vjp(gelu_tanh, up_sum)
    hidden = activated.astype(bf16)
    outcome = middle + live * (contract(hidden, full_down, ((1,), (0,))) + table[12])
    incoming = cotangent[0].astype(f32)
    grad_branch = (live * incoming).astype(bf16)
    grad_hidden = contract(grad_branch, full_down, ((1,), (1,)))
    grad_upsum = gelu_pull(grad_hidden)[0].astype(bf16)
    grad_normb = contract(grad_upsum, full_up, ((1,), (1,)))
    middle_part, gain_grad_b, shift_grad_b = norm_back(middle, table[10], grad_normb)
    grad_middle = incoming + middle_part
    grad_attn = (live * grad_middle).astype(bf16)
    grad_heads = contract(full_out, grad_attn, ((1,), (1,))).astype(bf16)
    grad_heads = grad_heads.reshape(groups, heads, HEAD, row_count)
    sending = [
        [row_major(at_group(grad_heads[:, h], here ^ step)) for step in range(groups)]
        for h in range(heads)
    ]
    arrived = []
    late = []
    parts = []
    for h in range(heads):
        pieces = swap_pieces(after(sending[h], arrived))
        arrived = pieces
        if h == 0:
            pieces = after(pieces, outcome)
        if late:
            if h > 1:
                for one in late:
                    one.receive(parts[-1])
            pieces = after(pieces, [one.send() for one in late])
        back = attend_back(lengths, here[None], *kept[h], pieces)
        if not late:
            hidden_late, grad_branch_late, grad_upsum_late, grad_attn_late = after(
                (hidden, grad_branch, grad_upsum, grad_attn), back
            )
            grad_down = contract(hidden_late, grad_branch_late, ((0,), (0,))).astype(bf16)
            grad_up = contract(normed_b, grad_upsum_late, ((0,), (0,))).astype(bf16)
            grad_out = contract(heads_out, grad_attn_late, ((1,), (0,))).astype(bf16)
            late = [Scatter(grad_down, True), Scatter(grad_up, False)]
        parts.append(back)
    grad_projected = []
    for back in parts:
        grad_projected.append(swap_pieces(back))
    grad_projected[:-1] = after(grad_projected[:-1], parts[-1])
    for one in late:
        one.receive(parts[-1])
    sent = [one.send() for one in late]

    whole = [in_order(pieces).reshape(groups * span, row_count) for pieces in grad_projected[:-1]]
    early = [row_major(contract(normed_a, part, ((0,), (1,))).astype(bf16)) for part in whole]
    early = Scatter(after(jnp.concatenate(early + [grad_out], axis=1), sent), True)
    pieces = after(grad_projected[-1], early.send())
    whole.append(in_order(pieces).reshape(groups * span, row_count))
    final = row_major(contract(normed_a, whole[-1], ((0,), (1,))).astype(bf16))
    grad_norma = sum(contract(part, weights, ((0,), (1,))) for part, weights in zip(whole, head_qkv))
    started = early.sent
    early.receive(whole[-1])
    sent = [early.send()]
    for one in late:
        one.receive(started)
        sent.append(one.send())
    grad_norma = after(grad_norma, sent)
    sums = [jnp.sum(part.astype(f32), axis=1) for part in whole]
    column_sums = by_kind(jnp.concatenate(sums)[None], groups)[0]
    start_part, gain_grad_a, shift_grad_a = norm_back(start, table[5], grad_norma)
    grad_start = grad_middle + start_part
    grad_embed = [
        jnp.sum(jnp.where(pass_of[:, index : index + 1], grad_start, 0.0), axis=0)
        for index in range(PASSES)
    ]
    vector_grads = jnp.stack(
        grad_embed
        + [
            gain_grad_a,
            shift_grad_a,
            column_sums[:width],
            column_sums[2 * width :],
            jnp.sum(grad_attn.astype(f32), axis=0),
            gain_grad_b,
            shift_grad_b,
            jnp.sum(grad_branch.astype(f32), axis=0),
        ]
    )
    bias_grads = jnp.sum(grad_upsum.astype(f32), axis=0)
    extra = [vector_grads.T.astype(bf16), bias_grads.reshape(width, ratio).astype(bf16)]
    last = Scatter(jnp.concatenate([final] + extra + [jnp.zeros((width, -small % 128), bf16)], axis=1), False)
    wave = 0
    tied = last.send()
    early.receive(tied)
    while last.order:
        sent = [early.send()] if early.order else []
        if wave % 2 == 0 and late[0].order:
            for one in late:
                one.receive(tied)
                sent.append(one.send())
        elif wave > 2 and not late[0].order:
            for one in late:
                one.receive(tied)
                sent.append(one.piece)
        last.receive(sent)
        tied = last.send()
        early.receive(tied)
        wave += 1
    last.receive()
    for one in late:
        one.receive(tied)
        one.finish()
    grad_down = late[0].piece
    grad_up = late[1].piece
    early = early.finish()
    grad_out = early[:, -width:]
    grad_qkv = [early[:, :-width], last.piece[:, : groups * span]]
    extra = last.piece[:, groups * span :].astype(f32)
    return (
        outcome.astype(bf16)[None],
        grad_start.astype(bf16)[None],
        by_kind(jnp.concatenate(grad_qkv, axis=1).astype(f32), groups),
        grad_out.astype(f32),
        grad_up.astype(f32),
        grad_down.astype(f32),
        extra[:, :vector_count].T,
        extra[:, vector_count:small].reshape(own * ratio),
    )


def solution(mesh):
    split = P(both, None)
    return jax.shard_map(
        on_device,
        mesh=mesh,
        in_specs=(
            P("seq", "blk", None),
            P("seq", "blk", None),
            P("seq", None),
            split,
            split,
            split,
            split,
            P(None, both),
            P(both),
        ),
        out_specs=(
            P("seq", "blk", None),
            P("seq", "blk", None),
            split,
            split,
            split,
            split,
            P(None, both),
            P(both),
        ),
        check_vma=False,
    )
```
